32 devices in a mesh: row: 4 (over z), col: 8 (over y, x, core).
Axes of the slice: x: 2, y: 2, z: 4, core: 2. Of those that a mesh axis runs over, the one named last changes fastest.
Arguments:
- gram: bfloat16 [2, 4, 256, 16, 8, 256], P(None, 'row', None, None, 'col'), as said below
Outputs:
- schur: float32 [2, 4, 256, 16, 8, 256], P(None, 'row', None, None, 'col')
Inputs may be any that keep to these rules, and one draw needn't show every extreme that they name: `gram`: the first 2048 columns of the slab form a symmetric matrix, and its leading 2 * 256 x 2 * 256 block is positive definite with smallest eigenvalue above 10.
All inputs are finite; a program needn't handle non-finite values.
Results may differ from the reference program's by a relative error of at most 0.0018.
Values may be sent and summed in bfloat16 or wider, within the bound.
No kernel may reach another device: no remote copies, remote signals or barrier semaphores. Data moves between devices by JAX's collectives and lax.ppermute only.
A program may use at most 64 MiB of HBM per device.

```python
import math
import jax
import jax.numpy as jnp

B = 256
ORDER = 32768
RT = 2
CT = 16
ROWS = 2048
N_ROW = 4
N_COL = 8


def draw_gram(key, part):
    first_key, second_key = jax.random.split(key)
    entries = jax.random.normal(first_key, (ROWS, ORDER), jnp.float32)
    square = entries[:, :ROWS]
    symmetric = (square + square.T) * math.sqrt(0.5)
    ridge = jax.random.uniform(second_key, (ROWS,), jnp.float32, 80.0, 160.0)
    symmetric = symmetric + jnp.diag(ridge)
    whole = jnp.concatenate([symmetric, entries[:, ROWS:]], axis=1)
    return whole.reshape(RT, N_ROW, B, CT, N_COL, B).astype(jnp.bfloat16)


def setup_inputs(seed: int = 0) -> dict:
    key_list = jax.random.split(jax.random.key(seed), 2)
    gram = draw_gram(jax.random.fold_in(key_list[1], 71), 0)
    return {"gram": gram}


def reference(gram):
    matrix = gram.astype(jnp.float32).reshape(ROWS, ORDER)
    column_tile = jnp.arange(ORDER) // B
    row_tile = jnp.arange(ROWS) // B
    for panel_index in range(2):
        panel_rows = matrix[panel_index * B:(panel_index + 1) * B]
        triangle = jnp.linalg.cholesky(panel_rows[:, panel_index * B:(panel_index + 1) * B])
        solved = jax.scipy.linalg.solve_triangular(triangle, panel_rows, lower=True)
        solved = jnp.where(column_tile[None, :] >= panel_index, solved, 0.0).astype(jnp.bfloat16)
        product = jnp.dot(solved[:, :ROWS].T.astype(jnp.float32), solved.astype(jnp.float32), preferred_element_type=jnp.float32)
        matrix = matrix - product
    retain = (row_tile >= 2)[:, None] & (column_tile >= 2)[None, :]
    result = jnp.where(retain, matrix, 0.0)
    return result.reshape(RT, N_ROW, B, CT, N_COL, B)
```

```python
import jax
import jax.numpy as jnp
from jax import lax
from jax.experimental import pallas as pl
from jax.experimental.pallas import tpu as pltpu
from jax.sharding import PartitionSpec as P

F32 = jnp.float32
BF16 = jnp.bfloat16
HIGHEST = lax.Precision.HIGHEST
NB = 64


def lane(x, j):
    return jnp.broadcast_to(x[:, j : j + 1], x.shape)


def sublane(x, j):
    return jnp.broadcast_to(x[j : j + 1, :], x.shape)


def inverse_factor(block):
    diagonal = lax.broadcasted_iota(jnp.int32, (NB, NB), 0) == lax.broadcasted_iota(jnp.int32, (NB, NB), 1)
    wide = jnp.concatenate([block, diagonal.astype(F32)], axis=1)
    groups = NB // 8
    sub = lax.broadcasted_iota(jnp.int32, (8, 2 * NB), 0)

    def group(g, tiles):
        pivot = tiles[0]
        cols = [lane(pivot, j) for j in range(8)]
        upper, recips, rows, scale = {}, [], [], None
        for j in range(8):
            d = sublane(cols[j], j)
            recips.append(1.0 / d)
            factor = jnp.where(sub > j, cols[j] * recips[j], 0.0)
            for l in range(j + 1, 8):
                upper[j, l] = sublane(cols[l], j)
                cols[l] = cols[l] - factor * upper[j, l]
            rows.append(sublane(pivot, j))
            pivot = pivot - factor * rows[j]
            root = lax.rsqrt(d)
            scale = root if scale is None else jnp.where(sub >= j, root, scale)
        out = []
        for i in range(1, groups):
            live = i < groups - g
            tile = tiles[i]
            own = [lane(tile, j) for j in range(8)]
            for j in range(8):
                factor = own[j] * recips[j]
                for l in range(j + 1, 8):
                    own[l] = own[l] - factor * upper[j, l]
                tile = tile - jnp.where(live, factor, 0.0) * rows[j]
            out.append(tile)
        out.append(pivot * scale)
        return tuple(pltpu.roll(t, 2 * NB - 8, 1) for t in out)

    tiles = tuple(wide[8 * i : 8 * i + 8] for i in range(groups))
    tiles = lax.fori_loop(0, groups, group, tiles)
    return jnp.concatenate(tiles, axis=0)[:, :NB]


def eliminate(work, inverse):
    size = work.shape[0]
    inverse[...] = (
        lax.broadcasted_iota(jnp.int32, (size, size), 0) == lax.broadcasted_iota(jnp.int32, (size, size), 1)
    ).astype(F32)
    for j in range(size // NB):
        lo, hi = j * NB, (j + 1) * NB
        own = inverse_factor(work[lo:hi, lo:hi])
        right = jnp.dot(own, work[lo:hi, :], precision=HIGHEST, preferred_element_type=F32)
        left = jnp.dot(own, inverse[lo:hi, :], precision=HIGHEST, preferred_element_type=F32)
        inverse[lo:hi, :] = left
        if hi < size:
            down = right[:, hi:].T
            work[hi:, :] -= jnp.dot(down, right, precision=HIGHEST, preferred_element_type=F32)
            inverse[hi:, :] -= jnp.dot(down, left, precision=HIGHEST, preferred_element_type=F32)


def split(x):
    high = x.astype(BF16)
    return high, (x - high.astype(F32)).astype(BF16)


def mm(a, b):
    return jnp.dot(a, b, preferred_element_type=F32)


def mmt(a, b):
    return lax.dot_general(a, b, (((1,), (1,)), ((), ())), preferred_element_type=F32)


def first_factor(corner, high_out, mid_out, work, inverse):
    work[...] = corner[...].astype(F32)
    eliminate(work, inverse)
    high, mid = split(inverse[...])
    high_out[...] = high
    mid_out[...] = mid


def second_factor(x0h, x0m, corner01, corner11, tiles0, tiles1, x1h_out, x1m_out, u01_out, rows_out, work, inverse):
    n_row = lax.axis_size("row")
    my_row = lax.axis_index("row")
    u01 = (mm(x0h[...], corner01[...]) + mm(x0m[...], corner01[...])).astype(BF16)
    u01_out[...] = u01
    work[...] = corner11[...].astype(F32) - mm(u01.T, u01)
    eliminate(work, inverse)
    high, mid = split(inverse[...])
    x1h_out[...] = high
    x1m_out[...] = mid
    size = high.shape[0]
    for slot in range(tiles0.shape[0]):
        row0 = (mmt(tiles0[slot], x0h[...]) + mmt(tiles0[slot], x0m[...])).astype(BF16)
        th, tm = split(tiles1[slot].astype(F32) - mm(row0, u01))
        row1 = mmt(th, high) + mmt(th, mid) + mmt(tm, high)
        row1 = jnp.where(slot * n_row + my_row >= 1, row1, 0.0)
        rows_out[slot, :, :size] = row0
        rows_out[slot, :, size:] = row1.astype(BF16)


def vmem_call(body, outs, scratch, name, flops):
    return pl.pallas_call(
        body,
        out_shape=outs,
        scratch_shapes=scratch,
        name=name,
        compiler_params=pltpu.CompilerParams(vmem_limit_bytes=24 << 20),
        cost_estimate=pl.CostEstimate(flops=flops, bytes_accessed=1 << 20, transcendentals=0),
    )


def update_chunk(chunk, sizes, hops, slabs, top, bottom, x0h, x0m, x1h, x1m, u01, rows, out):
    n_row = lax.axis_size("row")
    n_col = lax.axis_size("col")
    slots, cols, size, _ = slabs.shape
    width = sum(sizes)
    n_top, n_piece = len(top) // len(sizes), len(sizes)
    operands = [slabs, *top, *bottom, x0h, x0m, x1h, x1m, u01, rows]
    if out is not None:
        operands.append(out)
    n_wire = 1 + len(top) + len(bottom)
    halves = size // 128

    def body(*refs):
        slab_ref = refs[0]
        top_refs = refs[1 : 1 + len(top)]
        bottom_refs = refs[1 + len(top) : n_wire]
        x0h_ref, x0m_ref, x1h_ref, x1m_ref, u01_ref, rows_ref = refs[n_wire : n_wire + 6]
        out_ref, p0, p1, own, result, sems, out_sem = refs[len(operands) :]
        my_row = lax.axis_index("row")
        my_col = lax.axis_index("col")
        base = chunk * width
        own_copy = pltpu.make_async_copy(slab_ref.at[:, pl.ds(base, width)], own, sems.at[2])
        own_copy.start()

        def fetch(panel, target, sem, arrived):
            @pl.when(my_row == panel)
            def _():
                pltpu.make_async_copy(slab_ref.at[0, pl.ds(base, width)], target, sem).start()

            for way in range(n_top):
                here = 1 - panel if way == 0 else way + 1

                @pl.when(my_row == here)
                def _(way=way):
                    at = 0
                    for piece in range(n_piece):
                        pltpu.make_async_copy(
                            arrived[way * n_piece + piece], target.at[pl.ds(at, sizes[piece])], sem
                        ).start()
                        at += sizes[piece]

        fetch(0, p0, sems.at[0], top_refs)
        fetch(1, p1, sems.at[1], bottom_refs)
        pltpu.make_async_copy(slab_ref.at[0, pl.ds(base, width)], p0, sems.at[0]).wait()
        pltpu.make_async_copy(slab_ref.at[0, pl.ds(base, width)], p1, sems.at[1]).wait()
        own_copy.wait()
        for b in range(width):
            col_tile = (base + b) * n_col + my_col
            u0 = (mm(x0h_ref[...], p0[b]) + mm(x0m_ref[...], p0[b])).astype(BF16)
            th, tm = split(p1[b].astype(F32) - mm(u01_ref[...].T, u0))
            u1 = mm(x1h_ref[...], th) + mm(x1h_ref[...], tm) + mm(x1m_ref[...], th)
            u1 = jnp.where(col_tile >= 1, u1, 0.0).astype(BF16)
            both = jnp.concatenate([u0, u1], axis=0)
            for slot in range(slots):
                tile = own[slot, b].astype(F32) - mm(rows_ref[slot], both)
                keep = (slot * n_row + my_row >= 2) & (col_tile >= 2)
                tile = jnp.where(keep, tile, 0.0)
                for h in range(halves):
                    result[pl.ds(slot * size, size), b * halves + h, :] = tile[:, h * 128 : (h + 1) * 128]
        out_copy = pltpu.make_async_copy(result, out_ref.at[:, chunk], out_sem)
        out_copy.start()
        out_copy.wait()

    any_spec = pl.BlockSpec(memory_space=pl.ANY)
    vmem_spec = pl.BlockSpec(memory_space=pltpu.VMEM)
    specs = [any_spec] * n_wire + [vmem_spec] * 6 + ([any_spec] if out is not None else [])
    shape = (slots * size, cols // width, width * halves, 128)
    return pl.pallas_call(
        body,
        in_specs=specs,
        out_specs=any_spec,
        out_shape=jax.ShapeDtypeStruct(shape, F32),
        scratch_shapes=[
            pltpu.VMEM((width, size, size), BF16),
            pltpu.VMEM((width, size, size), BF16),
            pltpu.VMEM((slots, width, size, size), BF16),
            pltpu.VMEM((slots * size, width * halves, 128), F32),
            pltpu.SemaphoreType.DMA((3,)),
            pltpu.SemaphoreType.DMA,
        ],
        input_output_aliases={len(operands) - 1: 0} if out is not None else {},
        name="update",
        compiler_params=pltpu.CompilerParams(vmem_limit_bytes=24 << 20),
        cost_estimate=pl.CostEstimate(flops=2 * 10 * width * size**3, bytes_accessed=6 << 20, transcendentals=0),
    )(*operands)


def over_columns(x):
    n_col = lax.axis_size("col")
    my_col = lax.axis_index("col")
    step = 2
    while step < n_col:
        got = lax.ppermute(x, "col", [(i, i + step) for i in range(step) if i + step < n_col])
        x = jnp.where(my_col >= step, got, x)
        if 2 * step < n_col:
            pass
        step *= 2
    other = lax.ppermute(x, "col", [(i, i ^ 1) for i in range(n_col)])
    even = my_col % 2 == 0
    return jnp.where(even, x, other), jnp.where(even, other, x)


def local(gram):
    n_row = lax.axis_size("row")
    my_row = lax.axis_index("row")
    slots, _, size, cols, _, _ = gram.shape
    slabs = gram[:, 0, :, :, 0, :].transpose(0, 2, 1, 3)
    width = 4 if cols % 4 == 0 else cols
    chunks = [[width]] * (cols // width)
    chunks[0] = [1, width - 1]

    def up(x, source):
        return lax.ppermute(x, "row", [(source, source + 1)])

    pieces, at = [], 0
    for chunk in chunks:
        for count in chunk:
            pieces.append(slabs[0, at : at + count] if at else gram[0, 0, :, 0, 0, :][None])
            at += count
    swap = [lax.ppermute(p, "row", [(0, 1), (1, 0)]) for p in pieces]
    bottom_ways, top_ways = [swap], [swap]
    hop_b, hop_t = pieces, swap
    for source in range(1, n_row - 1):
        hop_b = [up(p, source) for p in hop_b]
        hop_t = [up(p, source) for p in hop_t]
        bottom_ways.append(hop_b)
        top_ways.append(hop_t)

    def here(panel, ways):
        x = pieces[0]
        for way, arrived in enumerate(ways):
            row = 1 - panel if way == 0 else way + 1
            x = jnp.where(my_row == row, arrived[0], x)
        return x[0]

    tiles0, tiles1 = over_columns(gram[:, 0, :, 0, 0, :])
    corner = jnp.stack([here(0, top_ways), here(1, bottom_ways)])
    corner0, corner1 = over_columns(corner)

    square = jax.ShapeDtypeStruct((size, size), BF16)
    scratch = [pltpu.VMEM((size, size), F32), pltpu.VMEM((size, size), F32)]
    x0h, x0m = vmem_call(first_factor, [square] * 2, scratch, "first", 1 << 30)(corner0[0])
    x1h, x1m, u01, rows = vmem_call(
        second_factor,
        [square] * 3 + [jax.ShapeDtypeStruct((slots, size, 2 * size), BF16)],
        scratch,
        "second",
        1 << 30,
    )(x0h, x0m, corner1[0], corner1[1], tiles0, tiles1)

    out, at = None, 0
    for chunk, sizes in enumerate(chunks):
        stop = at + len(sizes)
        top = [p for way in top_ways for p in way[at:stop]]
        bottom = [p for way in bottom_ways for p in way[at:stop]]
        out = update_chunk(chunk, sizes, n_row, slabs, top, bottom, x0h, x0m, x1h, x1m, u01, rows, out)
        at = stop
    return out.reshape(slots, 1, size, cols, 1, size)


def solution(mesh):
    spec = P(None, "row", None, None, "col", None)
    return jax.shard_map(local, mesh=mesh, in_specs=(spec,), out_specs=spec, check_vma=False)
```

```python
import jax
import jax.numpy as jnp
from jax import lax
from jax.experimental import pallas as pl
from jax.experimental.pallas import tpu as pltpu
from jax.sharding import PartitionSpec as P

F32 = jnp.float32
BF16 = jnp.bfloat16
HIGHEST = lax.Precision.HIGHEST
NB = 64


def lane(x, j):
    return jnp.broadcast_to(x[:, j : j + 1], x.shape)


def sublane(x, j):
    return jnp.broadcast_to(x[j : j + 1, :], x.shape)


def inverse_factor(block):
    diagonal = lax.broadcasted_iota(jnp.int32, (NB, NB), 0) == lax.broadcasted_iota(jnp.int32, (NB, NB), 1)
    wide = jnp.concatenate([block, diagonal.astype(F32)], axis=1)
    groups = NB // 8
    sub = lax.broadcasted_iota(jnp.int32, (8, 2 * NB), 0)

    def group(g, tiles):
        pivot = tiles[0]
        cols = [lane(pivot, j) for j in range(8)]
        upper, recips, rows, scale = {}, [], [], None
        for j in range(8):
            d = sublane(cols[j], j)
            recips.append(1.0 / d)
            factor = jnp.where(sub > j, cols[j] * recips[j], 0.0)
            for l in range(j + 1, 8):
                upper[j, l] = sublane(cols[l], j)
                cols[l] = cols[l] - factor * upper[j, l]
            rows.append(sublane(pivot, j))
            pivot = pivot - factor * rows[j]
            root = lax.rsqrt(d)
            scale = root if scale is None else jnp.where(sub >= j, root, scale)
        out = []
        for i in range(1, groups):
            live = i < groups - g
            tile = tiles[i]
            own = [lane(tile, j) for j in range(8)]
            for j in range(8):
                factor = own[j] * recips[j]
                for l in range(j + 1, 8):
                    own[l] = own[l] - factor * upper[j, l]
                tile = tile - jnp.where(live, factor, 0.0) * rows[j]
            out.append(tile)
        out.append(pivot * scale)
        return tuple(pltpu.roll(t, 2 * NB - 8, 1) for t in out)

    tiles = tuple(wide[8 * i : 8 * i + 8] for i in range(groups))
    tiles = lax.fori_loop(0, groups, group, tiles)
    return jnp.concatenate(tiles, axis=0)[:, :NB]


def eliminate(work, inverse):
    size = work.shape[0]
    inverse[...] = (
        lax.broadcasted_iota(jnp.int32, (size, size), 0) == lax.broadcasted_iota(jnp.int32, (size, size), 1)
    ).astype(F32)
    for j in range(size // NB):
        lo, hi = j * NB, (j + 1) * NB
        own = inverse_factor(work[lo:hi, lo:hi])
        right = jnp.dot(own, work[lo:hi, :], precision=HIGHEST, preferred_element_type=F32)
        left = jnp.dot(own, inverse[lo:hi, :], precision=HIGHEST, preferred_element_type=F32)
        inverse[lo:hi, :] = left
        if hi < size:
            down = right[:, hi:].T
            work[hi:, :] -= jnp.dot(down, right, precision=HIGHEST, preferred_element_type=F32)
            inverse[hi:, :] -= jnp.dot(down, left, precision=HIGHEST, preferred_element_type=F32)


def split(x):
    high = x.astype(BF16)
    return high, (x - high.astype(F32)).astype(BF16)


def mm(a, b):
    return jnp.dot(a, b, preferred_element_type=F32)


def mmt(a, b):
    return lax.dot_general(a, b, (((1,), (1,)), ((), ())), preferred_element_type=F32)


def from_column(column, mine, other, k):
    even = lax.axis_index("col") % 2 == column
    return jnp.where(even, mine[k].astype(F32), other[k].astype(F32))


def first_factor(mine, other, high_out, mid_out, work, inverse):
    work[...] = from_column(0, mine, other, 0)
    eliminate(work, inverse)
    high, mid = split(inverse[...])
    high_out[...] = high
    mid_out[...] = mid


def second_factor(x0h, x0m, mine, other, high_out, mid_out, u01_out, work, inverse):
    corner01 = from_column(1, mine, other, 0).astype(BF16)
    u01 = (mm(x0h[...], corner01) + mm(x0m[...], corner01)).astype(BF16)
    u01_out[...] = u01
    work[...] = from_column(1, mine, other, 1) - mm(u01.T, u01)
    eliminate(work, inverse)
    high, mid = split(inverse[...])
    high_out[...] = high
    mid_out[...] = mid


def row_factor(x0h, x0m, x1h, x1m, u01, mine, other, out):
    n_row = lax.axis_size("row")
    my_row = lax.axis_index("row")
    slots, size, _ = out.shape
    for slot in range(slots):
        tile0 = from_column(0, mine, other, slot).astype(BF16)
        row0 = (mmt(tile0, x0h[...]) + mmt(tile0, x0m[...])).astype(BF16)
        th, tm = split(from_column(1, mine, other, slot) - mm(row0, u01[...]))
        row1 = mmt(th, x1h[...]) + mmt(th, x1m[...]) + mmt(tm, x1h[...])
        row1 = jnp.where(slot * n_row + my_row >= 1, row1, 0.0)
        out[slot, :, :size] = row0
        out[slot, :, size:] = row1.astype(BF16)


def vmem_call(body, outs, scratch, name):
    return pl.pallas_call(
        body,
        out_shape=outs,
        scratch_shapes=scratch,
        name=name,
        compiler_params=pltpu.CompilerParams(vmem_limit_bytes=24 << 20),
        cost_estimate=pl.CostEstimate(flops=0, bytes_accessed=0, transcendentals=0),
    )


def update_chunk(base, width, slab0, slab1, top, bottom, x0h, x0m, x1h, x1m, u01, rows, out):
    n_row = lax.axis_size("row")
    n_col = lax.axis_size("col")
    cols, size, _ = slab0.shape
    slots = 1 + len(slab1)
    halves = size // 128
    wires = []
    for _, array, _, _ in top + bottom:
        if not any(array is w for w in wires):
            wires.append(array)

    def place(array):
        return next(i for i, w in enumerate(wires) if w is array)

    fetches = [
        [(row, place(array), first, count) for row, array, first, count in ways] for ways in (top, bottom)
    ]
    n_any = 1 + len(slab1) + len(wires)
    operands = [slab0, *slab1, *wires, x0h, x0m, x1h, x1m, u01, rows]
    if out is not None:
        operands.append(out)

    def body(*refs):
        slab_refs = refs[:slots]
        wire_refs = refs[slots:n_any]
        x0h_ref, x0m_ref, x1h_ref, x1m_ref, u01_ref, rows_ref = refs[n_any : n_any + 6]
        out_ref, p0, p1, own, result, sems, out_sem = refs[len(operands) :]
        my_row = lax.axis_index("row")
        my_col = lax.axis_index("col")
        for slot in range(slots):
            pltpu.make_async_copy(slab_refs[slot].at[pl.ds(base, width)], own.at[slot], sems.at[2 + slot]).start()
        for panel, target in enumerate((p0, p1)):

            @pl.when(my_row == panel)
            def _(panel=panel, target=target):
                pltpu.make_async_copy(slab_refs[0].at[pl.ds(base, width)], target, sems.at[panel]).start()

            for row in range(n_row):
                parts = [f[1:] for f in fetches[panel] if f[0] == row]
                if not parts:
                    continue

                @pl.when(my_row == row)
                def _(panel=panel, target=target, parts=parts):
                    at = 0
                    for wire, first, count in parts:
                        pltpu.make_async_copy(
                            wire_refs[wire].at[pl.ds(first, count)], target.at[pl.ds(at, count)], sems.at[panel]
                        ).start()
                        at += count

        for panel, target in enumerate((p0, p1)):
            pltpu.make_async_copy(slab_refs[0].at[pl.ds(base, width)], target, sems.at[panel]).wait()
        for slot in range(slots):
            pltpu.make_async_copy(slab_refs[slot].at[pl.ds(base, width)], own.at[slot], sems.at[2 + slot]).wait()
        for b in range(width):
            col_tile = (base + b) * n_col + my_col
            u0 = (mm(x0h_ref[...], p0[b]) + mm(x0m_ref[...], p0[b])).astype(BF16)
            th, tm = split(p1[b].astype(F32) - mm(u01_ref[...].T, u0))
            u1 = mm(x1h_ref[...], th) + mm(x1h_ref[...], tm) + mm(x1m_ref[...], th)
            u1 = jnp.where(col_tile >= 1, u1, 0.0).astype(BF16)
            both = jnp.concatenate([u0, u1], axis=0)
            for slot in range(slots):
                tile = own[slot, b].astype(F32) - mm(rows_ref[slot], both)
                keep = (slot * n_row + my_row >= 2) & (col_tile >= 2)
                tile = jnp.where(keep, tile, 0.0)
                for h in range(halves):
                    result[b, pl.ds(slot * size, size), h, :] = tile[:, h * 128 : (h + 1) * 128]
            pltpu.make_async_copy(result.at[b], out_ref.at[:, base + b], out_sem.at[b]).start()
        for b in range(width):
            pltpu.make_async_copy(result.at[b], out_ref.at[:, base + b], out_sem.at[b]).wait()

    any_spec = pl.BlockSpec(memory_space=pl.ANY)
    vmem_spec = pl.BlockSpec(memory_space=pltpu.VMEM)
    return pl.pallas_call(
        body,
        in_specs=[any_spec] * n_any + [vmem_spec] * 6 + ([any_spec] if out is not None else []),
        out_specs=any_spec,
        out_shape=jax.ShapeDtypeStruct((slots * size, cols, halves, 128), F32),
        scratch_shapes=[
            pltpu.VMEM((width, size, size), BF16),
            pltpu.VMEM((width, size, size), BF16),
            pltpu.VMEM((slots, width, size, size), BF16),
            pltpu.VMEM((width, slots * size, halves, 128), F32),
            pltpu.SemaphoreType.DMA((2 + slots,)),
            pltpu.SemaphoreType.DMA((width,)),
        ],
        input_output_aliases={len(operands) - 1: 0} if out is not None else {},
        name="update",
        compiler_params=pltpu.CompilerParams(vmem_limit_bytes=24 << 20),
        cost_estimate=pl.CostEstimate(flops=0, bytes_accessed=0, transcendentals=0),
    )(*operands)


def over_columns(name, tokens, x):
    n_col = lax.axis_size("col")
    my_col = lax.axis_index("col")
    tokens = list(tokens)
    step = 2
    while step < n_col:
        x = after(x, *(tokens.pop(0) if tokens else []))
        with jax.named_scope(f"{name}{step}"):
            got = lax.ppermute(x, "col", [(i, i + step) for i in range(step) if i + step < n_col])
        x = jnp.where(my_col >= step, got, x)
        step *= 2
    x = after(x, *(tokens.pop(0) if tokens else []))
    with jax.named_scope(f"{name}1"):
        return x, lax.ppermute(x, "col", [(i, i ^ 1) for i in range(n_col)])


def after(x, *tokens):
    return lax.optimization_barrier((x, *tokens))[0]


def local(gram):
    n_row = lax.axis_size("row")
    my_row = lax.axis_index("row")
    slots, _, size, cols, _, _ = gram.shape
    slab0 = gram[0, 0, :, :, 0, :].transpose(1, 0, 2)
    if cols % 8 == 0:
        first_counts = [1, cols // 2 - 1, cols // 2]
        second_counts = [1, 3] + [4] * (cols // 4 - 2) + [2, 2]
        widths = [4] * (cols // 4 - 1) + [2, 2]
    else:
        first_counts = second_counts = [1] * cols
        widths = [cols]

    def spans(counts):
        starts = [sum(counts[:i]) for i in range(len(counts))]
        return list(zip(starts, counts))

    corner_piece = gram[0, 0, :, 0, 0, :][None]
    cut = {(0, 1): corner_piece}
    for start, count in spans(first_counts) + spans(second_counts):
        if (start, count) not in cut:
            cut[start, count] = slab0[start : start + count]

    def send(name, x, *pairs):
        with jax.named_scope(name):
            return lax.ppermute(x, "row", [p for p in pairs])

    far_spans, near_spans = spans(first_counts), spans(second_counts)
    tile_rows = gram[:, 0, :, 0, 0, :]
    far = {s: send(f"far{s[0]}", cut[s], (0, 3), (1, 0)) for s in far_spans}
    near = {s: send(f"near{s[0]}", cut[s], (1, 2), (0, 1)) for s in near_spans[:2]}
    ready = [cut[s] for s in far_spans + near_spans[:2]]
    cross = send("cross", corner_piece, (0, 2), (1, 3))
    back = {}

    def tokens(i):
        return [d[s] for s in far_spans[i : i + 1] for d in (far, back) if s in d]

    top_ways = {1: near, 3: far, 2: {(0, 1): cross}}
    bottom_ways = {0: far, 2: near, 3: {(0, 1): cross}}
    hop_top, hop_bottom = {(0, 1): far[0, 1]}, {(0, 1): cross}
    for row in range(4, n_row):
        hop_top = {s: send(f"top{s[0]}", x, (row - 1, row)) for s, x in hop_top.items()}
        hop_bottom = {s: send(f"bottom{s[0]}", x, (row - 1, row)) for s, x in hop_bottom.items()}
        top_ways[row], bottom_ways[row] = hop_top, hop_bottom

    def here(ways):
        x = corner_piece
        for row, arrived in ways.items():
            x = jnp.where(my_row == row, arrived[0, 1], x)
        return x

    payload = jnp.concatenate([here(top_ways), here(bottom_ways)])
    corners = over_columns("corner", [], after(payload, tile_rows, *ready))

    square = jax.ShapeDtypeStruct((size, size), BF16)
    scratch = [pltpu.VMEM((size, size), F32), pltpu.VMEM((size, size), F32)]
    x0h, x0m = vmem_call(first_factor, [square] * 2, scratch, "first")(*corners)
    x1h, x1m, u01 = vmem_call(second_factor, [square] * 3, scratch, "second")(
        after(x0h, *tokens(1)), x0m, *corners
    )
    for i, s in enumerate(near_spans[2:]):
        gate = [x0h] if i < 2 else [x1h, near[near_spans[i - 1]]]
        near[s] = send(f"near{s[0]}", after(cut[s], *gate), (1, 2), (0, 1))
    back[0, 1] = cross
    for i, s in enumerate(far_spans[1:]):
        back[s] = send(f"back{s[0]}", after(far[s], x1h if i else x0h), (3, 2))
    on = {(0, 1): cross}
    for s in near_spans[1:3]:
        on[s] = send(f"on{s[0]}", after(near[s], x1h), (2, 3))
    tiles = over_columns("tiles", [[corners[0]], [], [x0h]], tile_rows)
    panels = jax.ShapeDtypeStruct((slots, size, 2 * size), BF16)
    rows = vmem_call(row_factor, panels, [], "rows")(after(x0h, on[near_spans[1]], *[back[s] for s in far_spans[1:2]], *[near[s] for s in near_spans[2:3]]), x0m, x1h, x1m, u01, *tiles)
    for s in near_spans[3:]:
        on[s] = send(f"on{s[0]}", after(near[s], rows), (2, 3))
    slab1 = [after(gram, x1h)[a, 0, :, :, 0, :].transpose(1, 0, 2) for a in range(1, slots)]

    top_ways, bottom_ways = {1: near, 3: far, 2: back}, {0: far, 2: near, 3: on}
    hop_top, hop_bottom = far, on
    for row in range(4, n_row):
        hop_top = {s: send(f"top{s[0]}", x, (row - 1, row)) for s, x in hop_top.items()}
        hop_bottom = {s: send(f"bottom{s[0]}", x, (row - 1, row)) for s, x in hop_bottom.items()}
        top_ways[row], bottom_ways[row] = hop_top, hop_bottom

    def parts(ways, base, width):
        out = []
        for row, arrived in ways.items():
            for (start, count), array in sorted(arrived.items(), key=lambda item: item[0]):
                lo, hi = max(start, base), min(start + count, base + width)
                if lo < hi:
                    out.append((row, array, lo - start, hi - lo))
        return out

    out = None
    for base, width in spans(widths):
        top, bottom = parts(top_ways, base, width), parts(bottom_ways, base, width)
        out = update_chunk(base, width, slab0, slab1, top, bottom, x0h, x0m, x1h, x1m, u01, rows, out)
    return out.reshape(slots, 1, size, cols, 1, size)


def solution(mesh):
    spec = P(None, "row", None, None, "col", None)
    return jax.shard_map(local, mesh=mesh, in_specs=(spec,), out_specs=spec, check_vma=False)
```

```python
import jax
import jax.numpy as jnp
from jax import lax
from jax.experimental import pallas as pl
from jax.experimental.pallas import tpu as pltpu
from jax.sharding import PartitionSpec as P

F32 = jnp.float32
BF16 = jnp.bfloat16
HIGHEST = lax.Precision.HIGHEST
NB = 64


def lane(x, j):
    return jnp.broadcast_to(x[:, j : j + 1], x.shape)


def sublane(x, j):
    return jnp.broadcast_to(x[j : j + 1, :], x.shape)


def inverse_factor(block):
    diagonal = lax.broadcasted_iota(jnp.int32, (NB, NB), 0) == lax.broadcasted_iota(jnp.int32, (NB, NB), 1)
    wide = jnp.concatenate([block, diagonal.astype(F32)], axis=1)
    groups = NB // 8
    sub = lax.broadcasted_iota(jnp.int32, (8, 2 * NB), 0)

    def group(g, tiles):
        pivot = tiles[0]
        cols = [lane(pivot, j) for j in range(8)]
        upper, recips, rows, scale = {}, [], [], None
        for j in range(8):
            d = sublane(cols[j], j)
            recips.append(1.0 / d)
            factor = jnp.where(sub > j, cols[j] * recips[j], 0.0)
            for l in range(j + 1, 8):
                upper[j, l] = sublane(cols[l], j)
                cols[l] = cols[l] - factor * upper[j, l]
            rows.append(sublane(pivot, j))
            pivot = pivot - factor * rows[j]
            root = lax.rsqrt(d)
            scale = root if scale is None else jnp.where(sub >= j, root, scale)
        out = []
        for i in range(1, groups):
            live = i < groups - g
            tile = tiles[i]
            own = [lane(tile, j) for j in range(8)]
            for j in range(8):
                factor = own[j] * recips[j]
                for l in range(j + 1, 8):
                    own[l] = own[l] - factor * upper[j, l]
                tile = tile - jnp.where(live, factor, 0.0) * rows[j]
            out.append(tile)
        out.append(pivot * scale)
        return tuple(pltpu.roll(t, 2 * NB - 8, 1) for t in out)

    tiles = tuple(wide[8 * i : 8 * i + 8] for i in range(groups))
    tiles = lax.fori_loop(0, groups, group, tiles)
    return jnp.concatenate(tiles, axis=0)[:, :NB]


def eliminate(work, inverse):
    size = work.shape[0]
    inverse[...] = (
        lax.broadcasted_iota(jnp.int32, (size, size), 0) == lax.broadcasted_iota(jnp.int32, (size, size), 1)
    ).astype(F32)
    for j in range(size // NB):
        lo, hi = j * NB, (j + 1) * NB
        own = inverse_factor(work[lo:hi, lo:hi])
        right = jnp.dot(own, work[lo:hi, :], precision=HIGHEST, preferred_element_type=F32)
        left = jnp.dot(own, inverse[lo:hi, :], precision=HIGHEST, preferred_element_type=F32)
        inverse[lo:hi, :] = left
        if hi < size:
            down = right[:, hi:].T
            work[hi:, :] -= jnp.dot(down, right, precision=HIGHEST, preferred_element_type=F32)
            inverse[hi:, :] -= jnp.dot(down, left, precision=HIGHEST, preferred_element_type=F32)


def split(x):
    high = x.astype(BF16)
    return high, (x - high.astype(F32)).astype(BF16)


def mm(a, b):
    return jnp.dot(a, b, preferred_element_type=F32)


def mmt(a, b):
    return lax.dot_general(a, b, (((1,), (1,)), ((), ())), preferred_element_type=F32)


def from_column(column, mine, other, k):
    even = lax.axis_index("col") % 2 == column
    return jnp.where(even, mine[k].astype(F32), other[k].astype(F32))


def first_factor(mine, other, high_out, mid_out, work, inverse):
    work[...] = from_column(0, mine, other, 0)
    eliminate(work, inverse)
    high, mid = split(inverse[...])
    high_out[...] = high
    mid_out[...] = mid


def second_factor(x0h, x0m, mine, other, high_out, mid_out, u01_out, work, inverse):
    corner01 = from_column(1, mine, other, 0).astype(BF16)
    u01 = (mm(x0h[...], corner01) + mm(x0m[...], corner01)).astype(BF16)
    u01_out[...] = u01.T
    work[...] = from_column(1, mine, other, 1) - mm(u01.T, u01)
    eliminate(work, inverse)
    high, mid = split(inverse[...])
    high_out[...] = high
    mid_out[...] = mid


def row_factor(x0h, x0m, x1h, x1m, u01, mine, other, out):
    n_row = lax.axis_size("row")
    my_row = lax.axis_index("row")
    slots, size, _ = out.shape
    for slot in range(slots):
        tile0 = from_column(0, mine, other, slot).astype(BF16)
        row0 = (mmt(tile0, x0h[...]) + mmt(tile0, x0m[...])).astype(BF16)
        th, tm = split(from_column(1, mine, other, slot) - mmt(row0, u01[...]))
        row1 = mmt(th, x1h[...]) + mmt(th, x1m[...]) + mmt(tm, x1h[...])
        row1 = jnp.where(slot * n_row + my_row >= 1, row1, 0.0)
        out[slot, :, :size] = row0
        out[slot, :, size:] = row1.astype(BF16)


def vmem_call(body, outs, scratch, name):
    return pl.pallas_call(
        body,
        out_shape=outs,
        scratch_shapes=scratch,
        name=name,
        compiler_params=pltpu.CompilerParams(vmem_limit_bytes=24 << 20),
        cost_estimate=pl.CostEstimate(flops=0, bytes_accessed=0, transcendentals=0),
    )


def update_chunk(base, width, slab0, slab1, top, bottom, x0h, x0m, x1h, x1m, u01, rows, out):
    n_row = lax.axis_size("row")
    n_col = lax.axis_size("col")
    cols, size, _ = slab0.shape
    slots = 1 + len(slab1)
    halves = size // 128
    wires = []
    for _, array, _, _ in top + bottom:
        if not any(array is w for w in wires):
            wires.append(array)

    def place(array):
        return next(i for i, w in enumerate(wires) if w is array)

    fetches = [
        [(row, place(array), first, count) for row, array, first, count in ways] for ways in (top, bottom)
    ]
    n_any = 1 + len(slab1) + len(wires)
    operands = [slab0, *slab1, *wires, x0h, x0m, x1h, x1m, u01, rows]
    if out is not None:
        operands.append(out)

    def body(*refs):
        slab_refs = refs[:slots]
        wire_refs = refs[slots:n_any]
        x0h_ref, x0m_ref, x1h_ref, x1m_ref, u01_ref, rows_ref = refs[n_any : n_any + 6]
        out_ref, p0, p1, own, result, sems, out_sem = refs[len(operands) :]
        my_row = lax.axis_index("row")
        my_col = lax.axis_index("col")
        for slot in range(slots):
            pltpu.make_async_copy(slab_refs[slot].at[pl.ds(base, width)], own.at[slot], sems.at[2 + slot]).start()
        for panel, target in enumerate((p0, p1)):

            @pl.when(my_row == panel)
            def _(panel=panel, target=target):
                pltpu.make_async_copy(slab_refs[0].at[pl.ds(base, width)], target, sems.at[panel]).start()

            for row in range(n_row):
                parts = [f[1:] for f in fetches[panel] if f[0] == row]
                if not parts:
                    continue

                @pl.when(my_row == row)
                def _(panel=panel, target=target, parts=parts):
                    at = 0
                    for wire, first, count in parts:
                        pltpu.make_async_copy(
                            wire_refs[wire].at[pl.ds(first, count)], target.at[pl.ds(at, count)], sems.at[panel]
                        ).start()
                        at += count

        for panel, target in enumerate((p0, p1)):
            pltpu.make_async_copy(slab_refs[0].at[pl.ds(base, width)], target, sems.at[panel]).wait()
        for slot in range(slots):
            pltpu.make_async_copy(slab_refs[slot].at[pl.ds(base, width)], own.at[slot], sems.at[2 + slot]).wait()
        wide0 = jnp.concatenate([p0[b] for b in range(width)], axis=1)
        wide1 = jnp.concatenate([p1[b] for b in range(width)], axis=1).astype(F32)
        pair = mm(jnp.concatenate([x0h_ref[...], x0m_ref[...]], axis=0), wide0)
        u0 = (pair[:size] + pair[size:]).astype(BF16)
        th, tm = split(wide1 - mm(u01_ref[...], u0))
        pair = mm(jnp.concatenate([x1h_ref[...], x1m_ref[...]], axis=0), th)
        u1 = pair[:size] + pair[size:] + mm(x1h_ref[...], tm)
        all_rows = jnp.concatenate([rows_ref[slot] for slot in range(slots)], axis=0)
        for b in range(width):
            col_tile = (base + b) * n_col + my_col
            span = slice(b * size, (b + 1) * size)
            second = jnp.where(col_tile >= 1, u1[:, span], 0.0).astype(BF16)
            product = mm(all_rows, jnp.concatenate([u0[:, span], second], axis=0))
            for slot in range(slots):
                tile = own[slot, b].astype(F32) - product[slot * size : (slot + 1) * size]
                keep = (slot * n_row + my_row >= 2) & (col_tile >= 2)
                tile = jnp.where(keep, tile, 0.0)
                for h in range(halves):
                    result[b, pl.ds(slot * size, size), h, :] = tile[:, h * 128 : (h + 1) * 128]
            pltpu.make_async_copy(result.at[b], out_ref.at[:, base + b], out_sem.at[b]).start()
        for b in range(width):
            pltpu.make_async_copy(result.at[b], out_ref.at[:, base + b], out_sem.at[b]).wait()

    any_spec = pl.BlockSpec(memory_space=pl.ANY)
    vmem_spec = pl.BlockSpec(memory_space=pltpu.VMEM)
    return pl.pallas_call(
        body,
        in_specs=[any_spec] * n_any + [vmem_spec] * 6 + ([any_spec] if out is not None else []),
        out_specs=any_spec,
        out_shape=jax.ShapeDtypeStruct((slots * size, cols, halves, 128), F32),
        scratch_shapes=[
            pltpu.VMEM((width, size, size), BF16),
            pltpu.VMEM((width, size, size), BF16),
            pltpu.VMEM((slots, width, size, size), BF16),
            pltpu.VMEM((width, slots * size, halves, 128), F32),
            pltpu.SemaphoreType.DMA((2 + slots,)),
            pltpu.SemaphoreType.DMA((width,)),
        ],
        input_output_aliases={len(operands) - 1: 0} if out is not None else {},
        name="update",
        compiler_params=pltpu.CompilerParams(vmem_limit_bytes=24 << 20),
        cost_estimate=pl.CostEstimate(flops=0, bytes_accessed=0, transcendentals=0),
    )(*operands)


def over_columns(name, tokens, x):
    n_col = lax.axis_size("col")
    my_col = lax.axis_index("col")
    tokens = list(tokens)
    step = 2
    while step < n_col:
        x = after(x, *(tokens.pop(0) if tokens else []))
        with jax.named_scope(f"{name}{step}"):
            got = lax.ppermute(x, "col", [(i, i + step) for i in range(step) if i + step < n_col])
        x = jnp.where(my_col >= step, got, x)
        step *= 2
    x = after(x, *(tokens.pop(0) if tokens else []))
    with jax.named_scope(f"{name}1"):
        return x, lax.ppermute(x, "col", [(i, i ^ 1) for i in range(n_col)])


def after(x, *tokens):
    return lax.optimization_barrier((x, *tokens))[0]


def local(gram):
    n_row = lax.axis_size("row")
    my_row = lax.axis_index("row")
    slots, _, size, cols, _, _ = gram.shape
    slab0 = gram[0, 0, :, :, 0, :].transpose(1, 0, 2)
    if cols % 8 == 0:
        first_counts = [1, cols // 2 - 1, cols // 2]
        second_counts = [1, 3] + [4] * (cols // 4 - 2) + [2, 2]
        widths = [4] * (cols // 4 - 1) + [2, 2]
    else:
        first_counts = second_counts = [1] * cols
        widths = [cols]

    def spans(counts):
        starts = [sum(counts[:i]) for i in range(len(counts))]
        return list(zip(starts, counts))

    corner_piece = gram[0, 0, :, 0, 0, :][None]
    cut = {(0, 1): corner_piece}
    for start, count in spans(first_counts) + spans(second_counts):
        if (start, count) not in cut:
            cut[start, count] = slab0[start : start + count]

    def send(name, x, *pairs):
        with jax.named_scope(name):
            return lax.ppermute(x, "row", [p for p in pairs])

    far_spans, near_spans = spans(first_counts), spans(second_counts)
    tile_rows = gram[:, 0, :, 0, 0, :]
    far, near, back, on = {}, {}, {}, {}
    top_ways, bottom_ways = {1: near, 3: far, 2: back}, {0: far, 2: near, 3: on}
    for row in range(4, n_row):
        top_ways[row], bottom_ways[row] = {}, {}

    def send_far(s, *tokens):
        far[s] = send(f"far{s[0]}", after(cut[s], *tokens), (0, 3), (1, 0))
        for row in range(4, n_row):
            top_ways[row][s] = send(f"top{row}_{s[0]}", top_ways[row - 1][s], (row - 1, row))

    def send_near(s, *tokens):
        near[s] = send(f"near{s[0]}", after(cut[s], *tokens), (1, 2), (0, 1))

    def send_back(s, *tokens):
        back[s] = send(f"back{s[0]}", after(far[s], *tokens), (3, 2))

    def send_on(s, *tokens):
        on[s] = send(f"on{s[0]}", after(near[s], *tokens), (2, 3))
        for row in range(4, n_row):
            bottom_ways[row][s] = send(f"bottom{row}_{s[0]}", bottom_ways[row - 1][s], (row - 1, row))

    def arrived(s):
        return [near[s]] if s in near else []

    corner_span = far_spans[0]
    send_far(corner_span)
    send_near(corner_span)
    back[corner_span] = on[corner_span] = send("cross", corner_piece, (0, 2), (1, 3))
    for row in range(4, n_row):
        x = bottom_ways[row - 1][corner_span]
        bottom_ways[row][corner_span] = send(f"bottom{row}", x, (row - 1, row))
    for s in near_spans[1:3]:
        send_near(s)

    def here(ways):
        x = corner_piece
        for row, pieces in ways.items():
            x = jnp.where(my_row == row, pieces[corner_span], x)
        return x

    payload = jnp.concatenate([here(top_ways), here(bottom_ways)])
    ready = [cut[s] for s in far_spans + near_spans[:3]]
    corners = over_columns("corner", [], after(payload, tile_rows, *ready))
    for s in far_spans[1:]:
        send_far(s)

    square = jax.ShapeDtypeStruct((size, size), BF16)
    scratch = [pltpu.VMEM((size, size), F32), pltpu.VMEM((size, size), F32)]
    x0h, x0m = vmem_call(first_factor, [square] * 2, scratch, "first")(*corners)
    for s in far_spans[1:2]:
        send_back(s, x0h)
    for s in near_spans[3:4]:
        send_near(s, x0h)
    second_gate = [far[s] for s in far_spans[1:2]]
    x1h, x1m, u01 = vmem_call(second_factor, [square] * 3, scratch, "second")(
        after(x0h, *second_gate), x0m, *corners
    )
    for i, s in enumerate(near_spans[4:]):
        send_near(s, x1h, near[near_spans[i + 1]])
    for s in far_spans[2:]:
        send_back(s, x1h)
    for s in near_spans[1:3]:
        send_on(s, x1h)
    tiles = over_columns("tiles", [[corners[0]], [], [x0h]], tile_rows)
    panels = jax.ShapeDtypeStruct((slots, size, 2 * size), BF16)
    rows_gate = [d[s] for d, k in ((on, near_spans[1:2]), (back, far_spans[1:2]), (near, near_spans[2:3])) for s in k]
    rows = vmem_call(row_factor, panels, [], "rows")(after(x0h, *rows_gate), x0m, x1h, x1m, u01, *tiles)
    slab1 = [after(gram, x1h)[a, 0, :, :, 0, :].transpose(1, 0, 2) for a in range(1, slots)]

    def parts(ways, base, width):
        found = []
        for row, pieces in ways.items():
            for (start, count), array in sorted(pieces.items(), key=lambda item: item[0]):
                lo, hi = max(start, base), min(start + count, base + width)
                if lo < hi:
                    found.append((row, array, lo - start, hi - lo))
        return found

    out = None
    waiting = [s for s in near_spans if s not in on]
    for base, width in spans(widths):
        top, bottom = parts(top_ways, base, width), parts(bottom_ways, base, width)
        out = update_chunk(base, width, slab0, slab1, top, bottom, x0h, x0m, x1h, x1m, u01, rows, out)
        for s in waiting[:1] if base == 0 else waiting:
            near[s], out = lax.optimization_barrier((near[s], out))
            send_on(s)
        waiting = waiting[1:] if base == 0 else []
    return out.reshape(slots, 1, size, cols, 1, size)


def solution(mesh):
    spec = P(None, "row", None, None, "col", None)
    return jax.shard_map(local, mesh=mesh, in_specs=(spec,), out_specs=spec, check_vma=False)
```

```python
import jax
import jax.numpy as jnp
from jax import lax
from jax.experimental import pallas as pl
from jax.experimental.pallas import tpu as pltpu
from jax.sharding import PartitionSpec as P

F32 = jnp.float32
BF16 = jnp.bfloat16
HIGHEST = lax.Precision.HIGHEST
NB = 64


def lane(x, j):
    return jnp.broadcast_to(x[:, j : j + 1], x.shape)


def sublane(x, j):
    return jnp.broadcast_to(x[j : j + 1, :], x.shape)


def inverse_factor(block):
    diagonal = lax.broadcasted_iota(jnp.int32, (NB, NB), 0) == lax.broadcasted_iota(jnp.int32, (NB, NB), 1)
    wide = jnp.concatenate([block, diagonal.astype(F32)], axis=1)
    groups = NB // 8
    sub = lax.broadcasted_iota(jnp.int32, (8, 2 * NB), 0)

    def group(g, tiles):
        pivot = tiles[0]
        cols = [lane(pivot, j) for j in range(8)]
        upper, recips, rows, scale = {}, [], [], None
        for j in range(8):
            d = sublane(cols[j], j)
            recips.append(1.0 / d)
            factor = jnp.where(sub > j, cols[j] * recips[j], 0.0)
            for l in range(j + 1, 8):
                upper[j, l] = sublane(cols[l], j)
                cols[l] = cols[l] - factor * upper[j, l]
            rows.append(sublane(pivot, j))
            pivot = pivot - factor * rows[j]
            root = lax.rsqrt(d)
            scale = root if scale is None else jnp.where(sub >= j, root, scale)
        out = []
        for i in range(1, groups):
            live = i < groups - g
            tile = tiles[i]
            own = [lane(tile, j) for j in range(8)]
            for j in range(8):
                factor = own[j] * recips[j]
                for l in range(j + 1, 8):
                    own[l] = own[l] - factor * upper[j, l]
                tile = tile - jnp.where(live, factor, 0.0) * rows[j]
            out.append(tile)
        out.append(pivot * scale)
        return tuple(pltpu.roll(t, 2 * NB - 8, 1) for t in out)

    tiles = tuple(wide[8 * i : 8 * i + 8] for i in range(groups))
    tiles = lax.fori_loop(0, groups, group, tiles)
    return jnp.concatenate(tiles, axis=0)[:, :NB]


def eliminate(work, inverse):
    size = work.shape[0]
    inverse[...] = (
        lax.broadcasted_iota(jnp.int32, (size, size), 0) == lax.broadcasted_iota(jnp.int32, (size, size), 1)
    ).astype(F32)
    for j in range(size // NB):
        lo, hi = j * NB, (j + 1) * NB
        own = inverse_factor(work[lo:hi, lo:hi])
        right = jnp.dot(own, work[lo:hi, :], precision=HIGHEST, preferred_element_type=F32)
        left = jnp.dot(own, inverse[lo:hi, :], precision=HIGHEST, preferred_element_type=F32)
        inverse[lo:hi, :] = left
        if hi < size:
            down = right[:, hi:].T
            work[hi:, :] -= jnp.dot(down, right, precision=HIGHEST, preferred_element_type=F32)
            inverse[hi:, :] -= jnp.dot(down, left, precision=HIGHEST, preferred_element_type=F32)


def split(x):
    high = x.astype(BF16)
    return high, (x - high.astype(F32)).astype(BF16)


def mm(a, b):
    return jnp.dot(a, b, preferred_element_type=F32)


def mmt(a, b):
    return lax.dot_general(a, b, (((1,), (1,)), ((), ())), preferred_element_type=F32)


def from_column(column, mine, other, k):
    even = lax.axis_index("col") % 2 == column
    return jnp.where(even, mine[k].astype(F32), other[k].astype(F32))


def first_factor(mine, other, high_out, mid_out, work, inverse):
    work[...] = from_column(0, mine, other, 0)
    eliminate(work, inverse)
    high, mid = split(inverse[...])
    high_out[...] = high
    mid_out[...] = mid


def second_factor(x0h, x0m, mine, other, high_out, mid_out, u01_out, work, inverse):
    corner01 = from_column(1, mine, other, 0).astype(BF16)
    u01 = (mm(x0h[...], corner01) + mm(x0m[...], corner01)).astype(BF16)
    u01_out[...] = u01.T
    work[...] = from_column(1, mine, other, 1) - mm(u01.T, u01)
    eliminate(work, inverse)
    high, mid = split(inverse[...])
    high_out[...] = high
    mid_out[...] = mid


def row_factor(x0h, x0m, x1h, x1m, u01, mine, other, out):
    n_row = lax.axis_size("row")
    my_row = lax.axis_index("row")
    slots, size, _ = out.shape
    for slot in range(slots):
        tile0 = from_column(0, mine, other, 2 + slot).astype(BF16)
        row0 = (mmt(tile0, x0h[...]) + mmt(tile0, x0m[...])).astype(BF16)
        th, tm = split(from_column(1, mine, other, 2 + slot) - mmt(row0, u01[...]))
        row1 = mmt(th, x1h[...]) + mmt(th, x1m[...]) + mmt(tm, x1h[...])
        row1 = jnp.where(slot * n_row + my_row >= 1, row1, 0.0)
        out[slot, :, :size] = row0
        out[slot, :, size:] = row1.astype(BF16)


def vmem_call(body, outs, scratch, name):
    return pl.pallas_call(
        body,
        out_shape=outs,
        scratch_shapes=scratch,
        name=name,
        compiler_params=pltpu.CompilerParams(vmem_limit_bytes=24 << 20),
        cost_estimate=pl.CostEstimate(flops=0, bytes_accessed=0, transcendentals=0),
    )


def update_chunk(base, width, slab0, slab1, top, bottom, x0h, x0m, x1h, x1m, u01, rows, out):
    n_row = lax.axis_size("row")
    n_col = lax.axis_size("col")
    cols, size, _ = slab0.shape
    slots = 1 + len(slab1)
    halves = size // 128
    wires = []
    for _, array, _, _ in top + bottom:
        if not any(array is w for w in wires):
            wires.append(array)

    def place(array):
        return next(i for i, w in enumerate(wires) if w is array)

    fetches = [
        [(row, place(array), first, count) for row, array, first, count in ways] for ways in (top, bottom)
    ]
    n_any = 1 + len(slab1) + len(wires)
    operands = [slab0, *slab1, *wires, x0h, x0m, x1h, x1m, u01, rows]
    if out is not None:
        operands.append(out)

    def body(*refs):
        slab_refs = refs[:slots]
        wire_refs = refs[slots:n_any]
        x0h_ref, x0m_ref, x1h_ref, x1m_ref, u01_ref, rows_ref = refs[n_any : n_any + 6]
        out_ref, p0, p1, own, result, sems, out_sem = refs[len(operands) :]
        my_row = lax.axis_index("row")
        my_col = lax.axis_index("col")
        for slot in range(slots):
            pltpu.make_async_copy(slab_refs[slot].at[pl.ds(base, width)], own.at[slot], sems.at[2 + slot]).start()
        for panel, target in enumerate((p0, p1)):

            @pl.when(my_row == panel)
            def _(panel=panel, target=target):
                pltpu.make_async_copy(slab_refs[0].at[pl.ds(base, width)], target, sems.at[panel]).start()

            for row in range(n_row):
                parts = [f[1:] for f in fetches[panel] if f[0] == row]
                if not parts:
                    continue

                @pl.when(my_row == row)
                def _(panel=panel, target=target, parts=parts):
                    at = 0
                    for wire, first, count in parts:
                        pltpu.make_async_copy(
                            wire_refs[wire].at[pl.ds(first, count)], target.at[pl.ds(at, count)], sems.at[panel]
                        ).start()
                        at += count

        for panel, target in enumerate((p0, p1)):
            pltpu.make_async_copy(slab_refs[0].at[pl.ds(base, width)], target, sems.at[panel]).wait()
        for slot in range(slots):
            pltpu.make_async_copy(slab_refs[slot].at[pl.ds(base, width)], own.at[slot], sems.at[2 + slot]).wait()
        wide0 = jnp.concatenate([p0[b] for b in range(width)], axis=1)
        wide1 = jnp.concatenate([p1[b] for b in range(width)], axis=1).astype(F32)
        pair = mm(jnp.concatenate([x0h_ref[...], x0m_ref[...]], axis=0), wide0)
        u0 = (pair[:size] + pair[size:]).astype(BF16)
        th, tm = split(wide1 - mm(u01_ref[...], u0))
        pair = mm(jnp.concatenate([x1h_ref[...], x1m_ref[...]], axis=0), th)
        u1 = pair[:size] + pair[size:] + mm(x1h_ref[...], tm)
        all_rows = jnp.concatenate([rows_ref[slot] for slot in range(slots)], axis=0)
        for b in range(width):
            col_tile = (base + b) * n_col + my_col
            span = slice(b * size, (b + 1) * size)
            second = jnp.where(col_tile >= 1, u1[:, span], 0.0).astype(BF16)
            product = mm(all_rows, jnp.concatenate([u0[:, span], second], axis=0))
            for slot in range(slots):
                tile = own[slot, b].astype(F32) - product[slot * size : (slot + 1) * size]
                keep = (slot * n_row + my_row >= 2) & (col_tile >= 2)
                tile = jnp.where(keep, tile, 0.0)
                for h in range(halves):
                    result[b, pl.ds(slot * size, size), h, :] = tile[:, h * 128 : (h + 1) * 128]
            pltpu.make_async_copy(result.at[b], out_ref.at[:, base + b], out_sem.at[b]).start()
        for b in range(width):
            pltpu.make_async_copy(result.at[b], out_ref.at[:, base + b], out_sem.at[b]).wait()

    any_spec = pl.BlockSpec(memory_space=pl.ANY)
    vmem_spec = pl.BlockSpec(memory_space=pltpu.VMEM)
    return pl.pallas_call(
        body,
        in_specs=[any_spec] * n_any + [vmem_spec] * 6 + ([any_spec] if out is not None else []),
        out_specs=any_spec,
        out_shape=jax.ShapeDtypeStruct((slots * size, cols, halves, 128), F32),
        scratch_shapes=[
            pltpu.VMEM((width, size, size), BF16),
            pltpu.VMEM((width, size, size), BF16),
            pltpu.VMEM((slots, width, size, size), BF16),
            pltpu.VMEM((width, slots * size, halves, 128), F32),
            pltpu.SemaphoreType.DMA((2 + slots,)),
            pltpu.SemaphoreType.DMA((width,)),
        ],
        input_output_aliases={len(operands) - 1: 0} if out is not None else {},
        name="update",
        compiler_params=pltpu.CompilerParams(vmem_limit_bytes=24 << 20),
        cost_estimate=pl.CostEstimate(flops=0, bytes_accessed=0, transcendentals=0),
    )(*operands)


def over_columns(name, tokens, x):
    n_col = lax.axis_size("col")
    my_col = lax.axis_index("col")
    tokens = list(tokens)
    step = 2
    while step < n_col:
        x = after(x, *(tokens.pop(0) if tokens else []))
        with jax.named_scope(f"{name}{step}"):
            got = lax.ppermute(x, "col", [(i, i + step) for i in range(step) if i + step < n_col])
        x = jnp.where(my_col >= step, got, x)
        step *= 2
    x = after(x, *(tokens.pop(0) if tokens else []))
    with jax.named_scope(f"{name}1"):
        return x, lax.ppermute(x, "col", [(i, i ^ 1) for i in range(n_col)])


def after(x, *tokens):
    return lax.optimization_barrier((x, *tokens))[0]


def local(gram):
    n_row = lax.axis_size("row")
    my_row = lax.axis_index("row")
    slots, _, size, cols, _, _ = gram.shape
    slab0 = gram[0, 0, :, :, 0, :].transpose(1, 0, 2)
    if cols % 8 == 0:
        first_counts = [1, cols // 2 - 1, cols // 2]
        second_counts = [1, 3] + [4] * (cols // 4 - 2) + [2, 2]
        widths = [4] * (cols // 4 - 1) + [2, 2]
    else:
        first_counts = second_counts = [1] * cols
        widths = [cols]

    def spans(counts):
        starts = [sum(counts[:i]) for i in range(len(counts))]
        return list(zip(starts, counts))

    corner_piece = gram[0, 0, :, 0, 0, :][None]
    cut = {(0, 1): corner_piece}
    for start, count in spans(first_counts) + spans(second_counts):
        if (start, count) not in cut:
            cut[start, count] = slab0[start : start + count]

    def send(name, x, *pairs):
        with jax.named_scope(name):
            return lax.ppermute(x, "row", [p for p in pairs])

    far_spans, near_spans = spans(first_counts), spans(second_counts)
    tile_rows = gram[:, 0, :, 0, 0, :]
    far, near, near_top, back, on = {}, {}, {}, {}, {}
    top_ways, bottom_ways = {1: near_top, 3: far, 2: back}, {0: far, 2: near, 3: on}
    for row in range(4, n_row):
        top_ways[row], bottom_ways[row] = {}, {}

    def send_far(s, *tokens):
        far[s] = send(f"far{s[0]}", after(cut[s], *tokens), (0, 3), (1, 0))
        for row in range(4, n_row) if s != far_spans[0] else ():
            top_ways[row][s] = send(f"top{row}_{s[0]}", top_ways[row - 1][s], (row - 1, row))

    def send_near(s, *tokens):
        near[s] = near_top[s] = send(f"near{s[0]}", after(cut[s], *tokens), (1, 2), (0, 1))

    def send_back(s, *tokens):
        back[s] = send(f"back{s[0]}", after(far[s], *tokens), (3, 2))

    def send_on(s, *tokens):
        on[s] = send(f"on{s[0]}", after(near[s], *tokens), (2, 3))
        for row in range(4, n_row):
            bottom_ways[row][s] = send(f"bottom{row}_{s[0]}", bottom_ways[row - 1][s], (row - 1, row))

    def arrived(s):
        return [near[s]] if s in near else []

    corner_span = far_spans[0]
    near_top[corner_span] = on[corner_span] = send("corner13", corner_piece, (1, 3), (0, 1))
    send_far(corner_span)
    top_piece = jnp.where(my_row == 0, corner_piece, jnp.where(my_row == 1, on[corner_span], far[corner_span]))
    bottom_piece = jnp.where(my_row == 0, far[corner_span], jnp.where(my_row == 1, corner_piece, on[corner_span]))
    pair = jnp.concatenate([top_piece, bottom_piece])
    got = send("pair", after(pair, *[cut[s] for s in far_spans[1:2]]), (3, 2))
    back[corner_span], near[corner_span] = got[:1], got[1:]
    pair = jnp.where(my_row == 2, got, pair)
    for row in range(4, n_row):
        got = send(f"pair{row}", pair, (row - 1, row))
        top_ways[row][corner_span], bottom_ways[row][corner_span] = got[:1], got[1:]
        pair = jnp.where(my_row == row, got, pair)
    for s in near_spans[1:3]:
        send_near(s)

    payload = jnp.concatenate([pair, tile_rows])
    ready = [cut[s] for s in far_spans + near_spans[:3]]
    for s in far_spans[1:]:
        send_far(s)
    corners = over_columns("corner", [[], *[[far[s]] for s in far_spans[1:3]]], after(payload, *ready))

    square = jax.ShapeDtypeStruct((size, size), BF16)
    scratch = [pltpu.VMEM((size, size), F32), pltpu.VMEM((size, size), F32)]
    x0h, x0m = vmem_call(first_factor, [square] * 2, scratch, "first")(*corners)
    for s in near_spans[3:4]:
        send_near(s, x0h)
    for s in far_spans[1:]:
        send_back(s, *[x0h] * (s != far_spans[1]))
    for s in near_spans[1:3]:
        send_on(s, x0h)
    second_gate = [d[s] for d, k in ((near, near_spans[2:3]), (back, far_spans[1:2])) for s in k]
    x1h, x1m, u01 = vmem_call(second_factor, [square] * 3, scratch, "second")(
        after(x0h, *second_gate), x0m, *corners
    )
    for i, s in enumerate(near_spans[4:]):
        send_near(s, near[near_spans[i + 2]], x1h)
    for s in near_spans[3:4]:
        send_on(s, x1h)
    panels = jax.ShapeDtypeStruct((slots, size, 2 * size), BF16)
    rows_gate = [d[s] for d, k in ((on, near_spans[2:3]),) for s in k]
    rows = vmem_call(row_factor, panels, [], "rows")(after(x0h, *rows_gate), x0m, x1h, x1m, u01, *corners)
    slab1 = [after(gram, x1h)[a, 0, :, :, 0, :].transpose(1, 0, 2) for a in range(1, slots)]

    def parts(ways, base, width):
        found = []
        for row, pieces in ways.items():
            for (start, count), array in sorted(pieces.items(), key=lambda item: item[0]):
                lo, hi = max(start, base), min(start + count, base + width)
                if lo < hi:
                    found.append((row, array, lo - start, hi - lo))
        return found

    out = None
    waiting = [s for s in near_spans if s not in on]
    for base, width in spans(widths):
        top, bottom = parts(top_ways, base, width), parts(bottom_ways, base, width)
        out = update_chunk(base, width, slab0, slab1, top, bottom, x0h, x0m, x1h, x1m, u01, rows, out)
        for s in waiting[:1]:
            near[s], out = lax.optimization_barrier((near[s], out))
            send_on(s)
        waiting = waiting[1:]
    return out.reshape(slots, 1, size, cols, 1, size)


def solution(mesh):
    spec = P(None, "row", None, None, "col", None)
    return jax.shard_map(local, mesh=mesh, in_specs=(spec,), out_specs=spec, check_vma=False)
```

```python
import jax
import jax.numpy as jnp
from jax import lax
from jax.experimental import pallas as pl
from jax.experimental.pallas import tpu as pltpu
from jax.sharding import PartitionSpec as P

F32 = jnp.float32
BF16 = jnp.bfloat16
HIGHEST = lax.Precision.HIGHEST
NB = 64


def lane(x, j):
    return jnp.broadcast_to(x[:, j : j + 1], x.shape)


def sublane(x, j):
    return jnp.broadcast_to(x[j : j + 1, :], x.shape)


def inverse_factor(block):
    diagonal = lax.broadcasted_iota(jnp.int32, (NB, NB), 0) == lax.broadcasted_iota(jnp.int32, (NB, NB), 1)
    wide = jnp.concatenate([block, diagonal.astype(F32)], axis=1)
    groups = NB // 8
    sub = lax.broadcasted_iota(jnp.int32, (8, 2 * NB), 0)

    def step(count):
        def group(g, tiles):
            pivot = tiles[0]
            cols = [lane(pivot, j) for j in range(8)]
            upper, recips, rows, scale = {}, [], [], None
            for j in range(8):
                d = sublane(cols[j], j)
                recips.append(1.0 / d)
                factor = jnp.where(sub > j, cols[j] * recips[j], 0.0)
                for l in range(j + 1, 8):
                    upper[j, l] = sublane(cols[l], j)
                    cols[l] = cols[l] - factor * upper[j, l]
                rows.append(sublane(pivot, j))
                pivot = pivot - factor * rows[j]
                root = lax.rsqrt(d)
                scale = root if scale is None else jnp.where(sub >= j, root, scale)
            out = []
            for i in range(1, count):
                live = i < groups - g
                tile = tiles[i]
                own = [lane(tile, j) for j in range(8)]
                for j in range(8):
                    factor = own[j] * recips[j]
                    for l in range(j + 1, 8):
                        own[l] = own[l] - factor * upper[j, l]
                    tile = tile - jnp.where(live, factor, 0.0) * rows[j]
                out.append(tile)
            out.append(pivot * scale)
            return tuple(pltpu.roll(t, 2 * NB - 8, 1) for t in out)

        return group

    half = groups // 2
    tiles = tuple(wide[8 * i : 8 * i + 8] for i in range(groups))
    tiles = lax.fori_loop(0, half, step(groups), tiles)
    rest = lax.fori_loop(half, groups, step(groups - half), tiles[: groups - half])
    done = [pltpu.roll(t, 2 * NB - 8 * (groups - half), 1) for t in tiles[groups - half :]]
    return jnp.concatenate([*done, *rest], axis=0)[:, :NB]


def eliminate(work, inverse):
    size = work.shape[0]
    inverse[...] = (
        lax.broadcasted_iota(jnp.int32, (size, size), 0) == lax.broadcasted_iota(jnp.int32, (size, size), 1)
    ).astype(F32)
    for j in range(size // NB):
        lo, hi = j * NB, (j + 1) * NB
        own = inverse_factor(work[lo:hi, lo:hi])
        right = jnp.dot(own, work[lo:hi, :], precision=HIGHEST, preferred_element_type=F32)
        left = jnp.dot(own, inverse[lo:hi, :], precision=HIGHEST, preferred_element_type=F32)
        inverse[lo:hi, :] = left
        if hi < size:
            down = right[:, hi:].T
            work[hi:, :] -= jnp.dot(down, right, precision=HIGHEST, preferred_element_type=F32)
            inverse[hi:, :] -= jnp.dot(down, left, precision=HIGHEST, preferred_element_type=F32)


def split(x):
    high = x.astype(BF16)
    return high, (x - high.astype(F32)).astype(BF16)


def mm(a, b):
    return jnp.dot(a, b, preferred_element_type=F32)


def mmt(a, b):
    return lax.dot_general(a, b, (((1,), (1,)), ((), ())), preferred_element_type=F32)


def from_column(column, mine, other, k):
    even = lax.axis_index("col") % 2 == column
    return jnp.where(even, mine[k].astype(F32), other[k].astype(F32))


def first_factor(mine, other, high_out, mid_out, work, inverse):
    work[...] = from_column(0, mine, other, 0)
    eliminate(work, inverse)
    high, mid = split(inverse[...])
    high_out[...] = high
    mid_out[...] = mid


def second_factor(x0h, x0m, mine, other, high_out, mid_out, u01_out, work, inverse):
    corner01 = from_column(1, mine, other, 0).astype(BF16)
    u01 = (mm(x0h[...], corner01) + mm(x0m[...], corner01)).astype(BF16)
    u01_out[...] = u01.T
    work[...] = from_column(1, mine, other, 1) - mm(u01.T, u01)
    eliminate(work, inverse)
    high, mid = split(inverse[...])
    high_out[...] = high
    mid_out[...] = mid


def row_factor(x0h, x0m, x1h, x1m, u01, mine, other, out):
    n_row = lax.axis_size("row")
    my_row = lax.axis_index("row")
    slots, size, _ = out.shape
    for slot in range(slots):
        tile0 = from_column(0, mine, other, 2 + slot).astype(BF16)
        row0 = (mmt(tile0, x0h[...]) + mmt(tile0, x0m[...])).astype(BF16)
        th, tm = split(from_column(1, mine, other, 2 + slot) - mmt(row0, u01[...]))
        row1 = mmt(th, x1h[...]) + mmt(th, x1m[...]) + mmt(tm, x1h[...])
        row1 = jnp.where(slot * n_row + my_row >= 1, row1, 0.0)
        out[slot, :, :size] = row0
        out[slot, :, size:] = row1.astype(BF16)


def vmem_call(body, outs, scratch, name):
    return pl.pallas_call(
        body,
        out_shape=outs,
        scratch_shapes=scratch,
        name=name,
        compiler_params=pltpu.CompilerParams(vmem_limit_bytes=24 << 20),
        cost_estimate=pl.CostEstimate(flops=0, bytes_accessed=0, transcendentals=0),
    )


def update_chunk(base, width, slab0, slab1, top, bottom, x0h, x0m, x1h, x1m, u01, rows, out):
    n_row = lax.axis_size("row")
    n_col = lax.axis_size("col")
    cols, size, _ = slab0.shape
    slots = 1 + len(slab1)
    halves = size // 128
    wires = []
    for _, array, _, _ in top + bottom:
        if not any(array is w for w in wires):
            wires.append(array)

    def place(array):
        return next(i for i, w in enumerate(wires) if w is array)

    fetches = [
        [(row, place(array), first, count) for row, array, first, count in ways] for ways in (top, bottom)
    ]
    n_any = 1 + len(slab1) + len(wires)
    operands = [slab0, *slab1, *wires, x0h, x0m, x1h, x1m, u01, rows]
    if out is not None:
        operands.append(out)

    def body(*refs):
        slab_refs = refs[:slots]
        wire_refs = refs[slots:n_any]
        x0h_ref, x0m_ref, x1h_ref, x1m_ref, u01_ref, rows_ref = refs[n_any : n_any + 6]
        out_ref, p0, p1, own, result, sems, out_sem = refs[len(operands) :]
        my_row = lax.axis_index("row")
        my_col = lax.axis_index("col")
        for slot in range(slots):
            pltpu.make_async_copy(slab_refs[slot].at[pl.ds(base, width)], own.at[slot], sems.at[2 + slot]).start()
        for panel, target in enumerate((p0, p1)):

            @pl.when(my_row == panel)
            def _(panel=panel, target=target):
                pltpu.make_async_copy(slab_refs[0].at[pl.ds(base, width)], target, sems.at[panel]).start()

            for row in range(n_row):
                parts = [f[1:] for f in fetches[panel] if f[0] == row]
                if not parts:
                    continue

                @pl.when(my_row == row)
                def _(panel=panel, target=target, parts=parts):
                    at = 0
                    for wire, first, count in parts:
                        pltpu.make_async_copy(
                            wire_refs[wire].at[pl.ds(first, count)], target.at[pl.ds(at, count)], sems.at[panel]
                        ).start()
                        at += count

        for panel, target in enumerate((p0, p1)):
            pltpu.make_async_copy(slab_refs[0].at[pl.ds(base, width)], target, sems.at[panel]).wait()
        for slot in range(slots):
            pltpu.make_async_copy(slab_refs[slot].at[pl.ds(base, width)], own.at[slot], sems.at[2 + slot]).wait()
        wide0 = jnp.concatenate([p0[b] for b in range(width)], axis=1)
        wide1 = jnp.concatenate([p1[b] for b in range(width)], axis=1).astype(F32)
        pair = mm(jnp.concatenate([x0h_ref[...], x0m_ref[...]], axis=0), wide0)
        u0 = (pair[:size] + pair[size:]).astype(BF16)
        th, tm = split(wide1 - mm(u01_ref[...], u0))
        pair = mm(jnp.concatenate([x1h_ref[...], x1m_ref[...]], axis=0), th)
        u1 = pair[:size] + pair[size:] + mm(x1h_ref[...], tm)
        all_rows = jnp.concatenate([rows_ref[slot] for slot in range(slots)], axis=0)
        for b in range(width):
            col_tile = (base + b) * n_col + my_col
            span = slice(b * size, (b + 1) * size)
            second = jnp.where(col_tile >= 1, u1[:, span], 0.0).astype(BF16)
            product = mm(all_rows, jnp.concatenate([u0[:, span], second], axis=0))
            for slot in range(slots):
                tile = own[slot, b].astype(F32) - product[slot * size : (slot + 1) * size]
                keep = (slot * n_row + my_row >= 2) & (col_tile >= 2)
                tile = jnp.where(keep, tile, 0.0)
                result[b, pl.ds(slot * size, size), :, :] = tile.reshape(size, halves, 128)
            pltpu.make_async_copy(result.at[b], out_ref.at[:, base + b], out_sem.at[b]).start()
        for b in range(width):
            pltpu.make_async_copy(result.at[b], out_ref.at[:, base + b], out_sem.at[b]).wait()

    any_spec = pl.BlockSpec(memory_space=pl.ANY)
    vmem_spec = pl.BlockSpec(memory_space=pltpu.VMEM)
    return pl.pallas_call(
        body,
        in_specs=[any_spec] * n_any + [vmem_spec] * 6 + ([any_spec] if out is not None else []),
        out_specs=any_spec,
        out_shape=jax.ShapeDtypeStruct((slots * size, cols, halves, 128), F32),
        scratch_shapes=[
            pltpu.VMEM((width, size, size), BF16),
            pltpu.VMEM((width, size, size), BF16),
            pltpu.VMEM((slots, width, size, size), BF16),
            pltpu.VMEM((width, slots * size, halves, 128), F32),
            pltpu.SemaphoreType.DMA((2 + slots,)),
            pltpu.SemaphoreType.DMA((width,)),
        ],
        input_output_aliases={len(operands) - 1: 0} if out is not None else {},
        name="update",
        compiler_params=pltpu.CompilerParams(vmem_limit_bytes=24 << 20),
        cost_estimate=pl.CostEstimate(flops=0, bytes_accessed=0, transcendentals=0),
    )(*operands)


def over_columns(name, tokens, x):
    n_col = lax.axis_size("col")
    my_col = lax.axis_index("col")
    tokens = list(tokens)
    step = 2
    while step < n_col:
        x = after(x, *(tokens.pop(0) if tokens else []))
        with jax.named_scope(f"{name}{step}"):
            got = lax.ppermute(x, "col", [(i, i + step) for i in range(step) if i + step < n_col])
        x = jnp.where(my_col >= step, got, x)
        step *= 2
    x = after(x, *(tokens.pop(0) if tokens else []))
    with jax.named_scope(f"{name}1"):
        return x, lax.ppermute(x, "col", [(i, i ^ 1) for i in range(n_col)])


def after(x, *tokens):
    return lax.optimization_barrier((x, *tokens))[0]


def local(gram):
    n_row = lax.axis_size("row")
    my_row = lax.axis_index("row")
    slots, _, size, cols, _, _ = gram.shape
    slab0 = gram[0, 0, :, :, 0, :].transpose(1, 0, 2)
    if cols % 8 == 0:
        first_counts = [1, cols // 2 - 1, cols // 2]
        second_counts = [1, 3] + [4] * (cols // 4 - 2) + [2, 2]
        widths = [4] * (cols // 4 - 1) + [2, 2]
    else:
        first_counts = second_counts = [1] * cols
        widths = [cols]

    def spans(counts):
        starts = [sum(counts[:i]) for i in range(len(counts))]
        return list(zip(starts, counts))

    corner_piece = gram[0, 0, :, 0, 0, :][None]
    cut = {(0, 1): corner_piece}
    for start, count in spans(first_counts) + spans(second_counts):
        if (start, count) not in cut:
            cut[start, count] = slab0[start : start + count]

    def send(name, x, *pairs):
        with jax.named_scope(name):
            return lax.ppermute(x, "row", [p for p in pairs])

    far_spans, near_spans = spans(first_counts), spans(second_counts)
    tile_rows = gram[:, 0, :, 0, 0, :]
    far, near, near_top, back, on = {}, {}, {}, {}, {}
    top_ways, bottom_ways = {1: near_top, 3: far, 2: back}, {0: far, 2: near, 3: on}
    for row in range(4, n_row):
        top_ways[row], bottom_ways[row] = {}, {}

    def send_far(s, *tokens):
        far[s] = send(f"far{s[0]}", after(cut[s], *tokens), (0, 3), (1, 0))
        for row in range(4, n_row) if s != far_spans[0] else ():
            top_ways[row][s] = send(f"top{row}_{s[0]}", top_ways[row - 1][s], (row - 1, row))

    def send_near(s, *tokens):
        near[s] = near_top[s] = send(f"near{s[0]}", after(cut[s], *tokens), (1, 2), (0, 1))

    def send_back(s, *tokens):
        back[s] = send(f"back{s[0]}", after(far[s], *tokens), (3, 2))

    def send_on(s, *tokens):
        on[s] = send(f"on{s[0]}", after(near[s], *tokens), (2, 3))
        for row in range(4, n_row):
            bottom_ways[row][s] = send(f"bottom{row}_{s[0]}", bottom_ways[row - 1][s], (row - 1, row))

    def arrived(s):
        return [near[s]] if s in near else []

    corner_span = far_spans[0]
    near_top[corner_span] = on[corner_span] = send("corner13", corner_piece, (1, 3), (0, 1))
    send_far(corner_span)
    top_piece = jnp.where(my_row == 0, corner_piece, jnp.where(my_row == 1, on[corner_span], far[corner_span]))
    bottom_piece = jnp.where(my_row == 0, far[corner_span], jnp.where(my_row == 1, corner_piece, on[corner_span]))
    pair = jnp.concatenate([top_piece, bottom_piece])
    got = send("pair", after(pair, *[cut[s] for s in far_spans[1:2]]), (3, 2))
    back[corner_span], near[corner_span] = got[:1], got[1:]
    pair = jnp.where(my_row == 2, got, pair)
    for row in range(4, n_row):
        got = send(f"pair{row}", pair, (row - 1, row))
        top_ways[row][corner_span], bottom_ways[row][corner_span] = got[:1], got[1:]
        pair = jnp.where(my_row == row, got, pair)
    for s in near_spans[1:3]:
        send_near(s)

    payload = jnp.concatenate([pair, tile_rows])
    ready = [cut[s] for s in far_spans + near_spans[:3]]
    for s in far_spans[1:]:
        send_far(s)
    corners = over_columns("corner", [[], *[[far[s]] for s in far_spans[1:3]]], after(payload, *ready))

    square = jax.ShapeDtypeStruct((size, size), BF16)
    scratch = [pltpu.VMEM((size, size), F32), pltpu.VMEM((size, size), F32)]
    x0h, x0m = vmem_call(first_factor, [square] * 2, scratch, "first")(*corners)
    for s in near_spans[3:4]:
        send_near(s, x0h)
    for s in far_spans[1:]:
        send_back(s, *[x0h] * (s != far_spans[1]))
    for s in near_spans[1:3]:
        send_on(s, x0h)
    second_gate = [d[s] for d, k in ((near, near_spans[2:3]), (back, far_spans[1:2])) for s in k]
    x1h, x1m, u01 = vmem_call(second_factor, [square] * 3, scratch, "second")(
        after(x0h, *second_gate), x0m, *corners
    )
    for i, s in enumerate(near_spans[4:]):
        send_near(s, near[near_spans[i + 2]], x1h)
    for s in near_spans[3:4]:
        send_on(s, x1h)
    panels = jax.ShapeDtypeStruct((slots, size, 2 * size), BF16)
    rows_gate = [d[s] for d, k in ((on, near_spans[2:3]),) for s in k]
    rows = vmem_call(row_factor, panels, [], "rows")(after(x0h, *rows_gate), x0m, x1h, x1m, u01, *corners)
    slab1 = [after(gram, x1h)[a, 0, :, :, 0, :].transpose(1, 0, 2) for a in range(1, slots)]

    def parts(ways, base, width):
        found = []
        for row, pieces in ways.items():
            for (start, count), array in sorted(pieces.items(), key=lambda item: item[0]):
                lo, hi = max(start, base), min(start + count, base + width)
                if lo < hi:
                    found.append((row, array, lo - start, hi - lo))
        return found

    out = None
    waiting = [s for s in near_spans if s not in on]
    for base, width in spans(widths):
        top, bottom = parts(top_ways, base, width), parts(bottom_ways, base, width)
        out = update_chunk(base, width, slab0, slab1, top, bottom, x0h, x0m, x1h, x1m, u01, rows, out)
        for s in waiting[:1]:
            near[s], out = lax.optimization_barrier((near[s], out))
            send_on(s)
        waiting = waiting[1:]
    return out.reshape(slots, 1, size, cols, 1, size)


def solution(mesh):
    spec = P(None, "row", None, None, "col", None)
    return jax.shard_map(local, mesh=mesh, in_specs=(spec,), out_specs=spec, check_vma=False)
```

```python
import jax
import jax.numpy as jnp
from jax import lax
from jax.experimental import pallas as pl
from jax.experimental.pallas import tpu as pltpu
from jax.sharding import PartitionSpec as P

F32 = jnp.float32
BF16 = jnp.bfloat16
HIGHEST = lax.Precision.HIGHEST
NB = 64


def lane(x, j):
    return jnp.broadcast_to(x[:, j : j + 1], x.shape)


def sublane(x, j):
    return jnp.broadcast_to(x[j : j + 1, :], x.shape)


def inverse_factor(block):
    diagonal = lax.broadcasted_iota(jnp.int32, (NB, NB), 0) == lax.broadcasted_iota(jnp.int32, (NB, NB), 1)
    wide = jnp.concatenate([block, diagonal.astype(F32)], axis=1)
    groups = NB // 8
    sub = lax.broadcasted_iota(jnp.int32, (8, 2 * NB), 0)

    def step(count):
        def group(g, tiles):
            pivot = tiles[0]
            cols = [lane(pivot, j) for j in range(8)]
            upper, recips, rows, scale = {}, [], [], None
            for j in range(8):
                d = sublane(cols[j], j)
                recips.append(1.0 / d)
                factor = jnp.where(sub > j, cols[j] * recips[j], 0.0)
                for l in range(j + 1, 8):
                    upper[j, l] = sublane(cols[l], j)
                    cols[l] = cols[l] - factor * upper[j, l]
                rows.append(sublane(pivot, j))
                pivot = pivot - factor * rows[j]
                root = lax.rsqrt(d)
                scale = root if scale is None else jnp.where(sub >= j, root, scale)
            out = []
            for i in range(1, count):
                live = i < groups - g
                tile = tiles[i]
                own = [lane(tile, j) for j in range(8)]
                for j in range(8):
                    factor = own[j] * recips[j]
                    for l in range(j + 1, 8):
                        own[l] = own[l] - factor * upper[j, l]
                    tile = tile - jnp.where(live, factor, 0.0) * rows[j]
                out.append(tile)
            out.append(pivot * scale)
            return tuple(pltpu.roll(t, 2 * NB - 8, 1) for t in out)

        return group

    half = groups // 2
    tiles = tuple(wide[8 * i : 8 * i + 8] for i in range(groups))
    tiles = lax.fori_loop(0, half, step(groups), tiles)
    rest = lax.fori_loop(half, groups, step(groups - half), tiles[: groups - half])
    done = [pltpu.roll(t, 2 * NB - 8 * (groups - half), 1) for t in tiles[groups - half :]]
    return jnp.concatenate([*done, *rest], axis=0)[:, :NB]


def eliminate(work, inverse):
    size = work.shape[0]
    inverse[...] = (
        lax.broadcasted_iota(jnp.int32, (size, size), 0) == lax.broadcasted_iota(jnp.int32, (size, size), 1)
    ).astype(F32)
    for j in range(size // NB):
        lo, hi = j * NB, (j + 1) * NB
        own = inverse_factor(work[lo:hi, lo:hi])
        right = jnp.dot(own, work[lo:hi, :], precision=HIGHEST, preferred_element_type=F32)
        left = jnp.dot(own, inverse[lo:hi, :], precision=HIGHEST, preferred_element_type=F32)
        inverse[lo:hi, :] = left
        if hi < size:
            down = right[:, hi:].T
            work[hi:, :] -= jnp.dot(down, right, precision=HIGHEST, preferred_element_type=F32)
            inverse[hi:, :] -= jnp.dot(down, left, precision=HIGHEST, preferred_element_type=F32)


def split(x):
    high = x.astype(BF16)
    return high, (x - high.astype(F32)).astype(BF16)


def mm(a, b):
    return jnp.dot(a, b, preferred_element_type=F32)


def mmt(a, b):
    return lax.dot_general(a, b, (((1,), (1,)), ((), ())), preferred_element_type=F32)


def from_column(column, mine, other, k):
    even = lax.axis_index("col") % 2 == column
    return jnp.where(even, mine[k].astype(F32), other[k].astype(F32))


def first_factor(mine, other, high_out, mid_out, work, inverse):
    work[...] = from_column(0, mine, other, 0)
    eliminate(work, inverse)
    high, mid = split(inverse[...])
    high_out[...] = high
    mid_out[...] = mid


def second_factor(x0h, x0m, mine, other, high_out, mid_out, u01_out, work, inverse):
    corner01 = from_column(1, mine, other, 0).astype(BF16)
    u01 = (mm(x0h[...], corner01) + mm(x0m[...], corner01)).astype(BF16)
    u01_out[...] = u01.T
    work[...] = from_column(1, mine, other, 1) - mm(u01.T, u01)
    eliminate(work, inverse)
    high, mid = split(inverse[...])
    high_out[...] = high
    mid_out[...] = mid


def row_factor(x0h, x0m, x1h, x1m, u01, mine, other, out):
    n_row = lax.axis_size("row")
    my_row = lax.axis_index("row")
    slots, size, _ = out.shape
    for slot in range(slots):
        tile0 = from_column(0, mine, other, 2 + slot).astype(BF16)
        row0 = (mmt(tile0, x0h[...]) + mmt(tile0, x0m[...])).astype(BF16)
        th, tm = split(from_column(1, mine, other, 2 + slot) - mmt(row0, u01[...]))
        row1 = mmt(th, x1h[...]) + mmt(th, x1m[...]) + mmt(tm, x1h[...])
        row1 = jnp.where(slot * n_row + my_row >= 1, row1, 0.0)
        out[slot, :, :size] = row0
        out[slot, :, size:] = row1.astype(BF16)


def vmem_call(body, outs, scratch, name):
    return pl.pallas_call(
        body,
        out_shape=outs,
        scratch_shapes=scratch,
        name=name,
        compiler_params=pltpu.CompilerParams(vmem_limit_bytes=24 << 20),
        cost_estimate=pl.CostEstimate(flops=0, bytes_accessed=0, transcendentals=0),
    )


def update_chunk(base, width, slab0, slab1, top, bottom, x0h, x0m, x1h, x1m, u01, rows, out):
    n_row = lax.axis_size("row")
    n_col = lax.axis_size("col")
    cols, size, _ = slab0.shape
    slots = 1 + len(slab1)
    halves = size // 128
    wires = []
    for _, array, _, _ in top + bottom:
        if not any(array is w for w in wires):
            wires.append(array)

    def place(array):
        return next(i for i, w in enumerate(wires) if w is array)

    fetches = [
        [(row, place(array), first, count) for row, array, first, count in ways] for ways in (top, bottom)
    ]
    n_any = 1 + len(slab1) + len(wires)
    operands = [slab0, *slab1, *wires, x0h, x0m, x1h, x1m, u01, rows]
    if out is not None:
        operands.append(out)

    def body(*refs):
        slab_refs = refs[:slots]
        wire_refs = refs[slots:n_any]
        x0h_ref, x0m_ref, x1h_ref, x1m_ref, u01_ref, rows_ref = refs[n_any : n_any + 6]
        out_ref, p0, p1, own, result, sems, out_sem = refs[len(operands) :]
        my_row = lax.axis_index("row")
        my_col = lax.axis_index("col")
        for slot in range(slots):
            pltpu.make_async_copy(slab_refs[slot].at[pl.ds(base, width)], own.at[slot], sems.at[2 + slot]).start()
        for panel, target in enumerate((p0, p1)):

            @pl.when(my_row == panel)
            def _(panel=panel, target=target):
                pltpu.make_async_copy(slab_refs[0].at[pl.ds(base, width)], target, sems.at[panel]).start()

            for row in range(n_row):
                parts = [f[1:] for f in fetches[panel] if f[0] == row]
                if not parts:
                    continue

                @pl.when(my_row == row)
                def _(panel=panel, target=target, parts=parts):
                    at = 0
                    for wire, first, count in parts:
                        pltpu.make_async_copy(
                            wire_refs[wire].at[pl.ds(first, count)], target.at[pl.ds(at, count)], sems.at[panel]
                        ).start()
                        at += count

        for panel, target in enumerate((p0, p1)):
            pltpu.make_async_copy(slab_refs[0].at[pl.ds(base, width)], target, sems.at[panel]).wait()
        for slot in range(slots):
            pltpu.make_async_copy(slab_refs[slot].at[pl.ds(base, width)], own.at[slot], sems.at[2 + slot]).wait()
        wide0 = jnp.concatenate([p0[b] for b in range(width)], axis=1)
        wide1 = jnp.concatenate([p1[b] for b in range(width)], axis=1).astype(F32)
        pair = mm(jnp.concatenate([x0h_ref[...], x0m_ref[...]], axis=0), wide0)
        u0 = (pair[:size] + pair[size:]).astype(BF16)
        th, tm = split(wide1 - mm(u01_ref[...], u0))
        pair = mm(jnp.concatenate([x1h_ref[...], x1m_ref[...]], axis=0), th)
        u1 = pair[:size] + pair[size:] + mm(x1h_ref[...], tm)
        all_rows = jnp.concatenate([rows_ref[slot] for slot in range(slots)], axis=0)
        for b in range(width):
            col_tile = (base + b) * n_col + my_col
            span = slice(b * size, (b + 1) * size)
            second = jnp.where(col_tile >= 1, u1[:, span], 0.0).astype(BF16)
            product = mm(all_rows, jnp.concatenate([u0[:, span], second], axis=0))
            for slot in range(slots):
                tile = own[slot, b].astype(F32) - product[slot * size : (slot + 1) * size]
                keep = (slot * n_row + my_row >= 2) & (col_tile >= 2)
                tile = jnp.where(keep, tile, 0.0)
                result[b, pl.ds(slot * size, size), :, :] = tile.reshape(size, halves, 128)
            pltpu.make_async_copy(result.at[b], out_ref.at[:, base + b], out_sem.at[b]).start()
        for b in range(width):
            pltpu.make_async_copy(result.at[b], out_ref.at[:, base + b], out_sem.at[b]).wait()

    any_spec = pl.BlockSpec(memory_space=pl.ANY)
    vmem_spec = pl.BlockSpec(memory_space=pltpu.VMEM)
    return pl.pallas_call(
        body,
        in_specs=[any_spec] * n_any + [vmem_spec] * 6 + ([any_spec] if out is not None else []),
        out_specs=any_spec,
        out_shape=jax.ShapeDtypeStruct((slots * size, cols, halves, 128), F32),
        scratch_shapes=[
            pltpu.VMEM((width, size, size), BF16),
            pltpu.VMEM((width, size, size), BF16),
            pltpu.VMEM((slots, width, size, size), BF16),
            pltpu.VMEM((width, slots * size, halves, 128), F32),
            pltpu.SemaphoreType.DMA((2 + slots,)),
            pltpu.SemaphoreType.DMA((width,)),
        ],
        input_output_aliases={len(operands) - 1: 0} if out is not None else {},
        name="update",
        compiler_params=pltpu.CompilerParams(vmem_limit_bytes=24 << 20),
        cost_estimate=pl.CostEstimate(flops=0, bytes_accessed=0, transcendentals=0),
    )(*operands)


def over_columns(name, tokens, x):
    n_col = lax.axis_size("col")
    my_col = lax.axis_index("col")
    tokens = list(tokens)
    step = 2
    while step < n_col:
        x = after(x, *(tokens.pop(0) if tokens else []))
        with jax.named_scope(f"{name}{step}"):
            got = lax.ppermute(x, "col", [(i, i + step) for i in range(step) if i + step < n_col])
        x = jnp.where(my_col >= step, got, x)
        step *= 2
    x = after(x, *(tokens.pop(0) if tokens else []))
    with jax.named_scope(f"{name}1"):
        return x, lax.ppermute(x, "col", [(i, i ^ 1) for i in range(n_col)])


def after(x, *tokens):
    return lax.optimization_barrier((x, *tokens))[0]


def local(gram):
    n_row = lax.axis_size("row")
    my_row = lax.axis_index("row")
    slots, _, size, cols, _, _ = gram.shape
    slab0 = gram[0, 0, :, :, 0, :].transpose(1, 0, 2)
    if cols % 8 == 0:
        first_counts = [1, cols // 2 - 1, cols // 2]
        second_counts = [1, 3] + [4] * (cols // 4 - 2) + [2, 2]
        widths = [4] * (cols // 4 - 1) + [2, 2]
    else:
        first_counts = second_counts = [1] * cols
        widths = [cols]

    def spans(counts):
        starts = [sum(counts[:i]) for i in range(len(counts))]
        return list(zip(starts, counts))

    corner_piece = gram[0, 0, :, 0, 0, :][None]
    cut = {(0, 1): corner_piece}
    for start, count in spans(first_counts) + spans(second_counts):
        if (start, count) not in cut:
            cut[start, count] = slab0[start : start + count]

    def send(name, x, *pairs):
        with jax.named_scope(name):
            return lax.ppermute(x, "row", [p for p in pairs])

    far_spans, near_spans = spans(first_counts), spans(second_counts)
    tile_rows = gram[:, 0, :, 0, 0, :]
    far, near, near_top, back, on = {}, {}, {}, {}, {}
    top_ways, bottom_ways = {1: near_top, 3: far, 2: back}, {0: far, 2: near, 3: on}
    for row in range(4, n_row):
        top_ways[row], bottom_ways[row] = {}, {}

    def send_far(s, *tokens):
        far[s] = send(f"far{s[0]}", after(cut[s], *tokens), (0, 3), (1, 0))
        for row in range(4, n_row) if s != far_spans[0] else ():
            top_ways[row][s] = send(f"top{row}_{s[0]}", top_ways[row - 1][s], (row - 1, row))

    def send_near(s, *tokens):
        near[s] = near_top[s] = send(f"near{s[0]}", after(cut[s], *tokens), (1, 2), (0, 1))

    def send_back(s, *tokens):
        back[s] = send(f"back{s[0]}", after(far[s], *tokens), (3, 2))

    def send_on(s, *tokens):
        on[s] = send(f"on{s[0]}", after(near[s], *tokens), (2, 3))
        for row in range(4, n_row):
            bottom_ways[row][s] = send(f"bottom{row}_{s[0]}", bottom_ways[row - 1][s], (row - 1, row))

    def arrived(s):
        return [near[s]] if s in near else []

    corner_span = far_spans[0]
    near_top[corner_span] = on[corner_span] = send("corner13", corner_piece, (1, 3), (0, 1))
    send_far(corner_span)
    top_piece = jnp.where(my_row == 0, corner_piece, jnp.where(my_row == 1, on[corner_span], far[corner_span]))
    bottom_piece = jnp.where(my_row == 0, far[corner_span], jnp.where(my_row == 1, corner_piece, on[corner_span]))
    pair = jnp.concatenate([top_piece, bottom_piece])
    got = send("pair", after(pair, *[cut[s] for s in far_spans[1:2]]), (3, 2))
    back[corner_span], near[corner_span] = got[:1], got[1:]
    pair = jnp.where(my_row == 2, got, pair)
    for row in range(4, n_row):
        got = send(f"pair{row}", pair, (row - 1, row))
        top_ways[row][corner_span], bottom_ways[row][corner_span] = got[:1], got[1:]
        pair = jnp.where(my_row == row, got, pair)
    for s in near_spans[1:3]:
        send_near(s)

    payload = jnp.concatenate([pair, tile_rows])
    ready = [cut[s] for s in far_spans + near_spans[:3]]
    for s in far_spans[1:]:
        send_far(s)
    slab1 = [after(gram, pair)[a, 0, :, :, 0, :].transpose(1, 0, 2) for a in range(1, slots)]
    gates = [[], *[[far[s]] for s in far_spans[1:3]]]
    gates[-1] += slab1
    corners = over_columns("corner", gates, after(payload, *ready))

    square = jax.ShapeDtypeStruct((size, size), BF16)
    scratch = [pltpu.VMEM((size, size), F32), pltpu.VMEM((size, size), F32)]
    x0h, x0m = vmem_call(first_factor, [square] * 2, scratch, "first")(*corners)
    for s in near_spans[3:4]:
        send_near(s, x0h)
    for s in far_spans[1:]:
        send_back(s, *[x0h] * (s != far_spans[1]))
    for s in near_spans[1:3]:
        send_on(s, x0h)
    second_gate = [d[s] for d, k in ((near, near_spans[2:3]), (back, far_spans[1:2])) for s in k]
    x1h, x1m, u01 = vmem_call(second_factor, [square] * 3, scratch, "second")(
        after(x0h, *second_gate), x0m, *corners
    )
    for i, s in enumerate(near_spans[4:]):
        send_near(s, near[near_spans[i + 2]], x1h)
    for s in near_spans[3:4]:
        send_on(s, x1h)
    panels = jax.ShapeDtypeStruct((slots, size, 2 * size), BF16)
    rows_gate = [d[s] for d, k in ((on, near_spans[2:3]),) for s in k]
    rows = vmem_call(row_factor, panels, [], "rows")(after(x0h, *rows_gate), x0m, x1h, x1m, u01, *corners)
    def parts(ways, base, width):
        found = []
        for row, pieces in ways.items():
            for (start, count), array in sorted(pieces.items(), key=lambda item: item[0]):
                lo, hi = max(start, base), min(start + count, base + width)
                if lo < hi:
                    found.append((row, array, lo - start, hi - lo))
        return found

    out = None
    waiting = [s for s in near_spans if s not in on]
    for base, width in spans(widths):
        top, bottom = parts(top_ways, base, width), parts(bottom_ways, base, width)
        out = update_chunk(base, width, slab0, slab1, top, bottom, x0h, x0m, x1h, x1m, u01, rows, out)
        for s in waiting[:1]:
            near[s], out = lax.optimization_barrier((near[s], out))
            send_on(s)
        waiting = waiting[1:]
    return out.reshape(slots, 1, size, cols, 1, size)


def solution(mesh):
    spec = P(None, "row", None, None, "col", None)
    return jax.shard_map(local, mesh=mesh, in_specs=(spec,), out_specs=spec, check_vma=False)
```

```python
import jax
import jax.numpy as jnp
from jax import lax
from jax.experimental import pallas as pl
from jax.experimental.pallas import tpu as pltpu
from jax.sharding import PartitionSpec as P

F32 = jnp.float32
BF16 = jnp.bfloat16
HIGHEST = lax.Precision.HIGHEST
NB = 64


def lane(x, j):
    return jnp.broadcast_to(x[:, j : j + 1], x.shape)


def sublane(x, j):
    return jnp.broadcast_to(x[j : j + 1, :], x.shape)


def inverse_factor(block):
    diagonal = lax.broadcasted_iota(jnp.int32, (NB, NB), 0) == lax.broadcasted_iota(jnp.int32, (NB, NB), 1)
    wide = jnp.concatenate([block, diagonal.astype(F32)], axis=1)
    groups = NB // 8
    sub = lax.broadcasted_iota(jnp.int32, (8, 2 * NB), 0)

    def step(count):
        def group(g, tiles):
            pivot = tiles[0]
            cols = [lane(pivot, j) for j in range(8)]
            upper, recips, rows, scale = {}, [], [], None
            for j in range(8):
                d = sublane(cols[j], j)
                recips.append(1.0 / d)
                factor = jnp.where(sub > j, cols[j] * recips[j], 0.0)
                for l in range(j + 1, 8):
                    upper[j, l] = sublane(cols[l], j)
                    cols[l] = cols[l] - factor * upper[j, l]
                rows.append(sublane(pivot, j))
                pivot = pivot - factor * rows[j]
                root = lax.rsqrt(d)
                scale = root if scale is None else jnp.where(sub >= j, root, scale)
            out = []
            for i in range(1, count):
                live = i < groups - g
                tile = tiles[i]
                own = [lane(tile, j) for j in range(8)]
                for j in range(8):
                    factor = own[j] * recips[j]
                    for l in range(j + 1, 8):
                        own[l] = own[l] - factor * upper[j, l]
                    tile = tile - jnp.where(live, factor, 0.0) * rows[j]
                out.append(tile)
            out.append(pivot * scale)
            return tuple(pltpu.roll(t, 2 * NB - 8, 1) for t in out)

        return group

    tiles, done, phase = tuple(wide[8 * i : 8 * i + 8] for i in range(groups)), [], groups // 4
    for start in range(0, groups, phase):
        left = groups - start
        tiles = lax.fori_loop(start, start + phase, step(left), tiles)
        done = [pltpu.roll(t, 2 * NB - 8 * phase, 1) for t in done] + list(tiles[left - phase :])
        tiles = tiles[: left - phase]
    return jnp.concatenate(done, axis=0)[:, :NB]


def eliminate(work, inverse):
    size = work.shape[0]
    inverse[...] = (
        lax.broadcasted_iota(jnp.int32, (size, size), 0) == lax.broadcasted_iota(jnp.int32, (size, size), 1)
    ).astype(F32)
    for j in range(size // NB):
        lo, hi = j * NB, (j + 1) * NB
        own = inverse_factor(work[lo:hi, lo:hi])
        right = jnp.dot(own, work[lo:hi, :], precision=HIGHEST, preferred_element_type=F32)
        left = jnp.dot(own, inverse[lo:hi, :], precision=HIGHEST, preferred_element_type=F32)
        inverse[lo:hi, :] = left
        if hi < size:
            down = right[:, hi:].T
            work[hi:, :] -= jnp.dot(down, right, precision=HIGHEST, preferred_element_type=F32)
            inverse[hi:, :] -= jnp.dot(down, left, precision=HIGHEST, preferred_element_type=F32)


def split(x):
    high = x.astype(BF16)
    return high, (x - high.astype(F32)).astype(BF16)


def mm(a, b):
    return jnp.dot(a, b, preferred_element_type=F32)


def mmt(a, b):
    return lax.dot_general(a, b, (((1,), (1,)), ((), ())), preferred_element_type=F32)


def from_column(column, mine, other, k):
    even = lax.axis_index("col") % 2 == column
    return jnp.where(even, mine[k].astype(F32), other[k].astype(F32))


def first_factor(mine, other, high_out, mid_out, work, inverse):
    work[...] = from_column(0, mine, other, 0)
    eliminate(work, inverse)
    high, mid = split(inverse[...])
    high_out[...] = high
    mid_out[...] = mid


def second_factor(x0h, x0m, mine, other, high_out, mid_out, u01_out, work, inverse):
    corner01 = from_column(1, mine, other, 0).astype(BF16)
    u01 = (mm(x0h[...], corner01) + mm(x0m[...], corner01)).astype(BF16)
    u01_out[...] = u01.T
    work[...] = from_column(1, mine, other, 1) - mm(u01.T, u01)
    eliminate(work, inverse)
    high, mid = split(inverse[...])
    high_out[...] = high
    mid_out[...] = mid


def row_factor(x0h, x0m, x1h, x1m, u01, mine, other, out):
    n_row = lax.axis_size("row")
    my_row = lax.axis_index("row")
    slots, size, _ = out.shape
    for slot in range(slots):
        tile0 = from_column(0, mine, other, 2 + slot).astype(BF16)
        row0 = (mmt(tile0, x0h[...]) + mmt(tile0, x0m[...])).astype(BF16)
        th, tm = split(from_column(1, mine, other, 2 + slot) - mmt(row0, u01[...]))
        row1 = mmt(th, x1h[...]) + mmt(th, x1m[...]) + mmt(tm, x1h[...])
        row1 = jnp.where(slot * n_row + my_row >= 1, row1, 0.0)
        out[slot, :, :size] = row0
        out[slot, :, size:] = row1.astype(BF16)


def vmem_call(body, outs, scratch, name):
    return pl.pallas_call(
        body,
        out_shape=outs,
        scratch_shapes=scratch,
        name=name,
        compiler_params=pltpu.CompilerParams(vmem_limit_bytes=24 << 20),
        cost_estimate=pl.CostEstimate(flops=0, bytes_accessed=0, transcendentals=0),
    )


def update_chunk(base, width, slab0, slab1, top, bottom, x0h, x0m, x1h, x1m, u01, rows, out):
    n_row = lax.axis_size("row")
    n_col = lax.axis_size("col")
    cols, size, _ = slab0.shape
    slots = 1 + len(slab1)
    halves = size // 128
    wires = []
    for _, array, _, _ in top + bottom:
        if not any(array is w for w in wires):
            wires.append(array)

    def place(array):
        return next(i for i, w in enumerate(wires) if w is array)

    fetches = [
        [(row, place(array), first, count) for row, array, first, count in ways] for ways in (top, bottom)
    ]
    n_any = 1 + len(slab1) + len(wires)
    operands = [slab0, *slab1, *wires, x0h, x0m, x1h, x1m, u01, rows]
    if out is not None:
        operands.append(out)

    def body(*refs):
        slab_refs = refs[:slots]
        wire_refs = refs[slots:n_any]
        x0h_ref, x0m_ref, x1h_ref, x1m_ref, u01_ref, rows_ref = refs[n_any : n_any + 6]
        out_ref, p0, p1, own, result, sems, out_sem = refs[len(operands) :]
        my_row = lax.axis_index("row")
        my_col = lax.axis_index("col")
        for slot in range(slots):
            pltpu.make_async_copy(slab_refs[slot].at[pl.ds(base, width)], own.at[slot], sems.at[2 + slot]).start()
        for panel, target in enumerate((p0, p1)):

            @pl.when(my_row == panel)
            def _(panel=panel, target=target):
                pltpu.make_async_copy(slab_refs[0].at[pl.ds(base, width)], target, sems.at[panel]).start()

            for row in range(n_row):
                parts = [f[1:] for f in fetches[panel] if f[0] == row]
                if not parts:
                    continue

                @pl.when(my_row == row)
                def _(panel=panel, target=target, parts=parts):
                    at = 0
                    for wire, first, count in parts:
                        pltpu.make_async_copy(
                            wire_refs[wire].at[pl.ds(first, count)], target.at[pl.ds(at, count)], sems.at[panel]
                        ).start()
                        at += count

        for panel, target in enumerate((p0, p1)):
            pltpu.make_async_copy(slab_refs[0].at[pl.ds(base, width)], target, sems.at[panel]).wait()
        for slot in range(slots):
            pltpu.make_async_copy(slab_refs[slot].at[pl.ds(base, width)], own.at[slot], sems.at[2 + slot]).wait()
        wide0 = jnp.concatenate([p0[b] for b in range(width)], axis=1)
        wide1 = jnp.concatenate([p1[b] for b in range(width)], axis=1).astype(F32)
        pair = mm(jnp.concatenate([x0h_ref[...], x0m_ref[...]], axis=0), wide0)
        u0 = (pair[:size] + pair[size:]).astype(BF16)
        th, tm = split(wide1 - mm(u01_ref[...], u0))
        pair = mm(jnp.concatenate([x1h_ref[...], x1m_ref[...]], axis=0), th)
        u1 = pair[:size] + pair[size:] + mm(x1h_ref[...], tm)
        all_rows = jnp.concatenate([rows_ref[slot] for slot in range(slots)], axis=0)
        for b in range(width):
            col_tile = (base + b) * n_col + my_col
            span = slice(b * size, (b + 1) * size)
            second = jnp.where(col_tile >= 1, u1[:, span], 0.0).astype(BF16)
            product = mm(all_rows, jnp.concatenate([u0[:, span], second], axis=0))
            for slot in range(slots):
                tile = own[slot, b].astype(F32) - product[slot * size : (slot + 1) * size]
                keep = (slot * n_row + my_row >= 2) & (col_tile >= 2)
                tile = jnp.where(keep, tile, 0.0)
                result[b, pl.ds(slot * size, size), :, :] = tile.reshape(size, halves, 128)
            pltpu.make_async_copy(result.at[b], out_ref.at[:, base + b], out_sem.at[b]).start()
        for b in range(width):
            pltpu.make_async_copy(result.at[b], out_ref.at[:, base + b], out_sem.at[b]).wait()

    any_spec = pl.BlockSpec(memory_space=pl.ANY)
    vmem_spec = pl.BlockSpec(memory_space=pltpu.VMEM)
    return pl.pallas_call(
        body,
        in_specs=[any_spec] * n_any + [vmem_spec] * 6 + ([any_spec] if out is not None else []),
        out_specs=any_spec,
        out_shape=jax.ShapeDtypeStruct((slots * size, cols, halves, 128), F32),
        scratch_shapes=[
            pltpu.VMEM((width, size, size), BF16),
            pltpu.VMEM((width, size, size), BF16),
            pltpu.VMEM((slots, width, size, size), BF16),
            pltpu.VMEM((width, slots * size, halves, 128), F32),
            pltpu.SemaphoreType.DMA((2 + slots,)),
            pltpu.SemaphoreType.DMA((width,)),
        ],
        input_output_aliases={len(operands) - 1: 0} if out is not None else {},
        name="update",
        compiler_params=pltpu.CompilerParams(vmem_limit_bytes=24 << 20),
        cost_estimate=pl.CostEstimate(flops=0, bytes_accessed=0, transcendentals=0),
    )(*operands)


def over_columns(name, tokens, x):
    n_col = lax.axis_size("col")
    my_col = lax.axis_index("col")
    tokens = list(tokens)
    step = 2
    while step < n_col:
        x = after(x, *(tokens.pop(0) if tokens else []))
        with jax.named_scope(f"{name}{step}"):
            got = lax.ppermute(x, "col", [(i, i + step) for i in range(step) if i + step < n_col])
        x = jnp.where(my_col >= step, got, x)
        step *= 2
    x = after(x, *(tokens.pop(0) if tokens else []))
    with jax.named_scope(f"{name}1"):
        return x, lax.ppermute(x, "col", [(i, i ^ 1) for i in range(n_col)])


def after(x, *tokens):
    return lax.optimization_barrier((x, *tokens))[0]


def local(gram):
    n_row = lax.axis_size("row")
    my_row = lax.axis_index("row")
    slots, _, size, cols, _, _ = gram.shape
    slab0 = gram[0, 0, :, :, 0, :].transpose(1, 0, 2)
    if cols % 8 == 0:
        first_counts = [1, cols // 2 - 1, cols // 2]
        second_counts = [1, 3] + [4] * (cols // 4 - 2) + [2, 2]
        widths = [4] * (cols // 4 - 1) + [2, 2]
    else:
        first_counts = second_counts = [1] * cols
        widths = [cols]

    def spans(counts):
        starts = [sum(counts[:i]) for i in range(len(counts))]
        return list(zip(starts, counts))

    corner_piece = gram[0, 0, :, 0, 0, :][None]
    cut = {(0, 1): corner_piece}
    for start, count in spans(first_counts) + spans(second_counts):
        if (start, count) not in cut:
            cut[start, count] = slab0[start : start + count]

    def send(name, x, *pairs):
        with jax.named_scope(name):
            return lax.ppermute(x, "row", [p for p in pairs])

    far_spans, near_spans = spans(first_counts), spans(second_counts)
    tile_rows = gram[:, 0, :, 0, 0, :]
    far, near, near_top, back, on = {}, {}, {}, {}, {}
    top_ways, bottom_ways = {1: near_top, 3: far, 2: back}, {0: far, 2: near, 3: on}
    for row in range(4, n_row):
        top_ways[row], bottom_ways[row] = {}, {}

    def send_far(s, *tokens):
        far[s] = send(f"far{s[0]}", after(cut[s], *tokens), (0, 3), (1, 0))
        for row in range(4, n_row) if s != far_spans[0] else ():
            top_ways[row][s] = send(f"top{row}_{s[0]}", top_ways[row - 1][s], (row - 1, row))

    def send_near(s, *tokens):
        near[s] = near_top[s] = send(f"near{s[0]}", after(cut[s], *tokens), (1, 2), (0, 1))

    def send_back(s, *tokens):
        back[s] = send(f"back{s[0]}", after(far[s], *tokens), (3, 2))

    def send_on(s, *tokens):
        on[s] = send(f"on{s[0]}", after(near[s], *tokens), (2, 3))
        for row in range(4, n_row):
            bottom_ways[row][s] = send(f"bottom{row}_{s[0]}", bottom_ways[row - 1][s], (row - 1, row))

    def arrived(s):
        return [near[s]] if s in near else []

    corner_span = far_spans[0]
    near_top[corner_span] = on[corner_span] = send("corner13", corner_piece, (1, 3), (0, 1))
    send_far(corner_span)
    top_piece = jnp.where(my_row == 0, corner_piece, jnp.where(my_row == 1, on[corner_span], far[corner_span]))
    bottom_piece = jnp.where(my_row == 0, far[corner_span], jnp.where(my_row == 1, corner_piece, on[corner_span]))
    pair = jnp.concatenate([top_piece, bottom_piece])
    got = send("pair", after(pair, *[cut[s] for s in far_spans[1:2]]), (3, 2))
    back[corner_span], near[corner_span] = (got, 0), (got, 1)
    pair = jnp.where(my_row == 2, got, pair)
    for row in range(4, n_row):
        got = send(f"pair{row}", pair, (row - 1, row))
        top_ways[row][corner_span], bottom_ways[row][corner_span] = got[:1], got[1:]
        pair = jnp.where(my_row == row, got, pair)
    for s in near_spans[1:3]:
        send_near(s)

    payload = jnp.concatenate([pair, tile_rows])
    ready = [cut[s] for s in far_spans + near_spans[:3]]
    for s in far_spans[1:]:
        send_far(s)
    slab1 = [after(gram, pair)[a, 0, :, :, 0, :].transpose(1, 0, 2) for a in range(1, slots)]
    gates = [[], *[[far[s]] for s in far_spans[1:3]]]
    gates[-1] += slab1
    gates[1] += [cut[s] for s in near_spans[4:]]
    corners = over_columns("corner", gates, after(payload, *ready))

    square = jax.ShapeDtypeStruct((size, size), BF16)
    scratch = [pltpu.VMEM((size, size), F32), pltpu.VMEM((size, size), F32)]
    x0h, x0m = vmem_call(first_factor, [square] * 2, scratch, "first")(*corners)
    for s in near_spans[3:4]:
        send_near(s, x0h)
    for s in far_spans[1:]:
        send_back(s, *[x0h] * (s != far_spans[1]))
    for s in near_spans[1:3]:
        send_on(s, x0h)
    second_gate = [d[s] for d, k in ((near, near_spans[2:3]), (back, far_spans[1:2])) for s in k]
    x1h, x1m, u01 = vmem_call(second_factor, [square] * 3, scratch, "second")(
        after(x0h, *second_gate), x0m, *corners
    )
    for i, s in enumerate(near_spans[4:]):
        send_near(s, near[near_spans[i + 2]], x1h)
    for s in near_spans[3:4]:
        send_on(s, x1h)
    panels = jax.ShapeDtypeStruct((slots, size, 2 * size), BF16)
    rows_gate = [d[s] for d, k in ((on, near_spans[2:3]),) for s in k]
    rows = vmem_call(row_factor, panels, [], "rows")(after(x0h, *rows_gate), x0m, x1h, x1m, u01, *corners)
    def parts(ways, base, width):
        found = []
        for row, pieces in ways.items():
            for (start, count), array in sorted(pieces.items(), key=lambda item: item[0]):
                array, shift = array if isinstance(array, tuple) else (array, 0)
                lo, hi = max(start, base), min(start + count, base + width)
                if lo < hi:
                    found.append((row, array, shift + lo - start, hi - lo))
        return found

    out = None
    waiting = [s for s in near_spans if s not in on]
    for base, width in spans(widths):
        top, bottom = parts(top_ways, base, width), parts(bottom_ways, base, width)
        out = update_chunk(base, width, slab0, slab1, top, bottom, x0h, x0m, x1h, x1m, u01, rows, out)
        for s in waiting[:1]:
            near[s], out = lax.optimization_barrier((near[s], out))
            send_on(s)
        waiting = waiting[1:]
    return out.reshape(slots, 1, size, cols, 1, size)


def solution(mesh):
    spec = P(None, "row", None, None, "col", None)
    return jax.shard_map(local, mesh=mesh, in_specs=(spec,), out_specs=spec, check_vma=False)
```

```python
import jax
import jax.numpy as jnp
from jax import lax
from jax.experimental import pallas as pl
from jax.experimental.pallas import tpu as pltpu
from jax.sharding import PartitionSpec as P

F32 = jnp.float32
BF16 = jnp.bfloat16
HIGHEST = lax.Precision.HIGHEST
NB = 64


def lane(x, j):
    return jnp.broadcast_to(x[:, j : j + 1], x.shape)


def sublane(x, j):
    return jnp.broadcast_to(x[j : j + 1, :], x.shape)


def inverse_factor(block):
    diagonal = lax.broadcasted_iota(jnp.int32, (NB, NB), 0) == lax.broadcasted_iota(jnp.int32, (NB, NB), 1)
    wide = jnp.concatenate([block, diagonal.astype(F32)], axis=1)
    groups = NB // 8
    sub = lax.broadcasted_iota(jnp.int32, (8, 2 * NB), 0)

    def step(count):
        def group(g, tiles):
            pivot = tiles[0]
            cols = [lane(pivot, j) for j in range(8)]
            upper, recips, rows, scale = {}, [], [], None
            for j in range(8):
                d = sublane(cols[j], j)
                recips.append(1.0 / d)
                factor = jnp.where(sub > j, cols[j] * recips[j], 0.0)
                for l in range(j + 1, 8):
                    upper[j, l] = sublane(cols[l], j)
                    cols[l] = cols[l] - factor * upper[j, l]
                rows.append(sublane(pivot, j))
                pivot = pivot - factor * rows[j]
                root = lax.rsqrt(d)
                scale = root if scale is None else jnp.where(sub >= j, root, scale)
            out = []
            for i in range(1, count):
                live = i < groups - g
                tile = tiles[i]
                own = [lane(tile, j) for j in range(8)]
                for j in range(8):
                    factor = own[j] * recips[j]
                    for l in range(j + 1, 8):
                        own[l] = own[l] - factor * upper[j, l]
                    tile = tile - jnp.where(live, factor, 0.0) * rows[j]
                out.append(tile)
            out.append(pivot * scale)
            return tuple(pltpu.roll(t, 2 * NB - 8, 1) for t in out)

        return group

    tiles, done, phase = tuple(wide[8 * i : 8 * i + 8] for i in range(groups)), [], groups // 4
    for start in range(0, groups, phase):
        left = groups - start
        tiles = lax.fori_loop(start, start + phase, step(left), tiles)
        done = [pltpu.roll(t, 2 * NB - 8 * phase, 1) for t in done] + list(tiles[left - phase :])
        tiles = tiles[: left - phase]
    return jnp.concatenate(done, axis=0)[:, :NB]


def eliminate(work, inverse):
    size = work.shape[0]
    inverse[...] = (
        lax.broadcasted_iota(jnp.int32, (size, size), 0) == lax.broadcasted_iota(jnp.int32, (size, size), 1)
    ).astype(F32)
    for j in range(size // NB):
        lo, hi = j * NB, (j + 1) * NB
        own = inverse_factor(work[lo:hi, lo:hi])
        cut, top = hi // 128 * 128, -(-hi // 128) * 128
        left = jnp.dot(own, inverse[lo:hi, :top], precision=HIGHEST, preferred_element_type=F32)
        inverse[lo:hi, :top] = left
        if hi < size:
            right = jnp.dot(own, work[lo:hi, cut:], precision=HIGHEST, preferred_element_type=F32)
            down = right[:, hi - cut :].T
            work[hi:, cut:] -= jnp.dot(down, right, precision=HIGHEST, preferred_element_type=F32)
            inverse[hi:, :top] -= jnp.dot(down, left, precision=HIGHEST, preferred_element_type=F32)


def split(x):
    high = x.astype(BF16)
    return high, (x - high.astype(F32)).astype(BF16)


def mm(a, b):
    return jnp.dot(a, b, preferred_element_type=F32)


def mmt(a, b):
    return lax.dot_general(a, b, (((1,), (1,)), ((), ())), preferred_element_type=F32)


def from_column(column, mine, other, k):
    even = lax.axis_index("col") % 2 == column
    return jnp.where(even, mine[k].astype(F32), other[k].astype(F32))


def first_factor(mine, other, high_out, mid_out, work, inverse):
    work[...] = from_column(0, mine, other, 0)
    eliminate(work, inverse)
    high, mid = split(inverse[...])
    high_out[...] = high
    mid_out[...] = mid


def second_factor(x0h, x0m, mine, other, high_out, mid_out, u01_out, work, inverse):
    corner01 = from_column(1, mine, other, 0).astype(BF16)
    u01 = (mm(x0h[...], corner01) + mm(x0m[...], corner01)).astype(BF16)
    u01_out[...] = u01.T
    work[...] = from_column(1, mine, other, 1) - mm(u01.T, u01)
    eliminate(work, inverse)
    high, mid = split(inverse[...])
    high_out[...] = high
    mid_out[...] = mid


def row_factor(x0h, x0m, x1h, x1m, u01, mine, other, out):
    n_row = lax.axis_size("row")
    my_row = lax.axis_index("row")
    slots, size, _ = out.shape
    for slot in range(slots):
        tile0 = from_column(0, mine, other, 2 + slot).astype(BF16)
        row0 = (mmt(tile0, x0h[...]) + mmt(tile0, x0m[...])).astype(BF16)
        th, tm = split(from_column(1, mine, other, 2 + slot) - mmt(row0, u01[...]))
        row1 = mmt(th, x1h[...]) + mmt(th, x1m[...]) + mmt(tm, x1h[...])
        row1 = jnp.where(slot * n_row + my_row >= 1, row1, 0.0)
        out[slot, :, :size] = row0
        out[slot, :, size:] = row1.astype(BF16)


def vmem_call(body, outs, scratch, name):
    return pl.pallas_call(
        body,
        out_shape=outs,
        scratch_shapes=scratch,
        name=name,
        compiler_params=pltpu.CompilerParams(vmem_limit_bytes=24 << 20),
        cost_estimate=pl.CostEstimate(flops=0, bytes_accessed=0, transcendentals=0),
    )


def update_chunk(base, width, slab0, slab1, top, bottom, x0h, x0m, x1h, x1m, u01, rows, out):
    n_row = lax.axis_size("row")
    n_col = lax.axis_size("col")
    cols, size, _ = slab0.shape
    slots = 1 + len(slab1)
    halves = size // 128
    wires = []
    for _, array, _, _ in top + bottom:
        if not any(array is w for w in wires):
            wires.append(array)

    def place(array):
        return next(i for i, w in enumerate(wires) if w is array)

    fetches = [
        [(row, place(array), first, count) for row, array, first, count in ways] for ways in (top, bottom)
    ]
    n_any = 1 + len(slab1) + len(wires)
    operands = [slab0, *slab1, *wires, x0h, x0m, x1h, x1m, u01, rows]
    if out is not None:
        operands.append(out)

    def body(*refs):
        slab_refs = refs[:slots]
        wire_refs = refs[slots:n_any]
        x0h_ref, x0m_ref, x1h_ref, x1m_ref, u01_ref, rows_ref = refs[n_any : n_any + 6]
        out_ref, p0, p1, own, result, sems, out_sem = refs[len(operands) :]
        my_row = lax.axis_index("row")
        my_col = lax.axis_index("col")
        for slot in range(slots):
            pltpu.make_async_copy(slab_refs[slot].at[pl.ds(base, width)], own.at[slot], sems.at[2 + slot]).start()
        for panel, target in enumerate((p0, p1)):

            @pl.when(my_row == panel)
            def _(panel=panel, target=target):
                pltpu.make_async_copy(slab_refs[0].at[pl.ds(base, width)], target, sems.at[panel]).start()

            for row in range(n_row):
                parts = [f[1:] for f in fetches[panel] if f[0] == row]
                if not parts:
                    continue

                @pl.when(my_row == row)
                def _(panel=panel, target=target, parts=parts):
                    at = 0
                    for wire, first, count in parts:
                        pltpu.make_async_copy(
                            wire_refs[wire].at[pl.ds(first, count)], target.at[pl.ds(at, count)], sems.at[panel]
                        ).start()
                        at += count

        for panel, target in enumerate((p0, p1)):
            pltpu.make_async_copy(slab_refs[0].at[pl.ds(base, width)], target, sems.at[panel]).wait()
        for slot in range(slots):
            pltpu.make_async_copy(slab_refs[slot].at[pl.ds(base, width)], own.at[slot], sems.at[2 + slot]).wait()
        wide0 = jnp.concatenate([p0[b] for b in range(width)], axis=1)
        wide1 = jnp.concatenate([p1[b] for b in range(width)], axis=1).astype(F32)
        pair = mm(jnp.concatenate([x0h_ref[...], x0m_ref[...]], axis=0), wide0)
        u0 = (pair[:size] + pair[size:]).astype(BF16)
        th, tm = split(wide1 - mm(u01_ref[...], u0))
        pair = mm(jnp.concatenate([x1h_ref[...], x1m_ref[...]], axis=0), th)
        u1 = pair[:size] + pair[size:] + mm(x1h_ref[...], tm)
        all_rows = jnp.concatenate([rows_ref[slot] for slot in range(slots)], axis=0)
        for b in range(width):
            col_tile = (base + b) * n_col + my_col
            span = slice(b * size, (b + 1) * size)
            second = jnp.where(col_tile >= 1, u1[:, span], 0.0).astype(BF16)
            product = mm(all_rows, jnp.concatenate([u0[:, span], second], axis=0))
            for slot in range(slots):
                tile = own[slot, b].astype(F32) - product[slot * size : (slot + 1) * size]
                keep = (slot * n_row + my_row >= 2) & (col_tile >= 2)
                tile = jnp.where(keep, tile, 0.0)
                result[b, pl.ds(slot * size, size), :, :] = tile.reshape(size, halves, 128)
            pltpu.make_async_copy(result.at[b], out_ref.at[:, base + b], out_sem.at[b]).start()
        for b in range(width):
            pltpu.make_async_copy(result.at[b], out_ref.at[:, base + b], out_sem.at[b]).wait()

    any_spec = pl.BlockSpec(memory_space=pl.ANY)
    vmem_spec = pl.BlockSpec(memory_space=pltpu.VMEM)
    return pl.pallas_call(
        body,
        in_specs=[any_spec] * n_any + [vmem_spec] * 6 + ([any_spec] if out is not None else []),
        out_specs=any_spec,
        out_shape=jax.ShapeDtypeStruct((slots * size, cols, halves, 128), F32),
        scratch_shapes=[
            pltpu.VMEM((width, size, size), BF16),
            pltpu.VMEM((width, size, size), BF16),
            pltpu.VMEM((slots, width, size, size), BF16),
            pltpu.VMEM((width, slots * size, halves, 128), F32),
            pltpu.SemaphoreType.DMA((2 + slots,)),
            pltpu.SemaphoreType.DMA((width,)),
        ],
        input_output_aliases={len(operands) - 1: 0} if out is not None else {},
        name="update",
        compiler_params=pltpu.CompilerParams(vmem_limit_bytes=24 << 20),
        cost_estimate=pl.CostEstimate(flops=0, bytes_accessed=0, transcendentals=0),
    )(*operands)


def over_columns(name, tokens, x):
    n_col = lax.axis_size("col")
    my_col = lax.axis_index("col")
    tokens = list(tokens)
    step = 2
    while step < n_col:
        x = after(x, *(tokens.pop(0) if tokens else []))
        with jax.named_scope(f"{name}{step}"):
            got = lax.ppermute(x, "col", [(i, i + step) for i in range(step) if i + step < n_col])
        x = jnp.where(my_col >= step, got, x)
        step *= 2
    x = after(x, *(tokens.pop(0) if tokens else []))
    with jax.named_scope(f"{name}1"):
        return x, lax.ppermute(x, "col", [(i, i ^ 1) for i in range(n_col)])


def after(x, *tokens):
    return lax.optimization_barrier((x, *tokens))[0]


def local(gram):
    n_row = lax.axis_size("row")
    my_row = lax.axis_index("row")
    slots, _, size, cols, _, _ = gram.shape
    slab0 = gram[0, 0, :, :, 0, :].transpose(1, 0, 2)
    if cols % 8 == 0:
        first_counts = [1, cols // 2 - 1, cols // 2]
        second_counts = [1, 3] + [4] * (cols // 4 - 2) + [2, 2]
        widths = [4] * (cols // 4 - 1) + [2, 2]
    else:
        first_counts = second_counts = [1] * cols
        widths = [cols]

    def spans(counts):
        starts = [sum(counts[:i]) for i in range(len(counts))]
        return list(zip(starts, counts))

    corner_piece = gram[0, 0, :, 0, 0, :][None]
    cut = {(0, 1): corner_piece}
    for start, count in spans(first_counts) + spans(second_counts):
        if (start, count) not in cut:
            cut[start, count] = slab0[start : start + count]

    def send(name, x, *pairs):
        with jax.named_scope(name):
            return lax.ppermute(x, "row", [p for p in pairs])

    far_spans, near_spans = spans(first_counts), spans(second_counts)
    tile_rows = gram[:, 0, :, 0, 0, :]
    far, near, near_top, back, on = {}, {}, {}, {}, {}
    top_ways, bottom_ways = {1: near_top, 3: far, 2: back}, {0: far, 2: near, 3: on}
    for row in range(4, n_row):
        top_ways[row], bottom_ways[row] = {}, {}

    def send_far(s, *tokens):
        far[s] = send(f"far{s[0]}", after(cut[s], *tokens), (0, 3), (1, 0))
        for row in range(4, n_row) if s != far_spans[0] else ():
            top_ways[row][s] = send(f"top{row}_{s[0]}", top_ways[row - 1][s], (row - 1, row))

    def send_near(s, *tokens):
        near[s] = near_top[s] = send(f"near{s[0]}", after(cut[s], *tokens), (1, 2), (0, 1))

    def send_back(s, *tokens):
        back[s] = send(f"back{s[0]}", after(far[s], *tokens), (3, 2))

    def send_on(s, *tokens):
        on[s] = send(f"on{s[0]}", after(near[s], *tokens), (2, 3))
        for row in range(4, n_row):
            bottom_ways[row][s] = send(f"bottom{row}_{s[0]}", bottom_ways[row - 1][s], (row - 1, row))

    def arrived(s):
        return [near[s]] if s in near else []

    corner_span = far_spans[0]
    near_top[corner_span] = on[corner_span] = send("corner13", corner_piece, (1, 3), (0, 1))
    send_far(corner_span)
    top_piece = jnp.where(my_row == 0, corner_piece, jnp.where(my_row == 1, on[corner_span], far[corner_span]))
    bottom_piece = jnp.where(my_row == 0, far[corner_span], jnp.where(my_row == 1, corner_piece, on[corner_span]))
    pair = jnp.concatenate([top_piece, bottom_piece])
    got = send("pair", after(pair, *[cut[s] for s in far_spans[1:2]]), (3, 2))
    back[corner_span], near[corner_span] = (got, 0), (got, 1)
    pair = jnp.where(my_row == 2, got, pair)
    for row in range(4, n_row):
        got = send(f"pair{row}", pair, (row - 1, row))
        top_ways[row][corner_span], bottom_ways[row][corner_span] = got[:1], got[1:]
        pair = jnp.where(my_row == row, got, pair)
    for s in near_spans[1:3]:
        send_near(s)

    payload = jnp.concatenate([pair, tile_rows])
    ready = [cut[s] for s in far_spans + near_spans[:3]]
    for s in far_spans[1:]:
        send_far(s)
    slab1 = [after(gram, pair)[a, 0, :, :, 0, :].transpose(1, 0, 2) for a in range(1, slots)]
    gates = [[], *[[far[s]] for s in far_spans[1:3]]]
    gates[-1] += slab1
    gates[1] += [cut[s] for s in near_spans[4:]]
    corners = over_columns("corner", gates, after(payload, *ready))

    square = jax.ShapeDtypeStruct((size, size), BF16)
    scratch = [pltpu.VMEM((size, size), F32), pltpu.VMEM((size, size), F32)]
    x0h, x0m = vmem_call(first_factor, [square] * 2, scratch, "first")(*corners)
    for s in near_spans[3:4]:
        send_near(s, x0h)
    for s in far_spans[1:]:
        send_back(s, *[x0h] * (s != far_spans[1]))
    for s in near_spans[1:3]:
        send_on(s, x0h)
    second_gate = [d[s] for d, k in ((near, near_spans[2:3]), (back, far_spans[1:2])) for s in k]
    x1h, x1m, u01 = vmem_call(second_factor, [square] * 3, scratch, "second")(
        after(x0h, *second_gate), x0m, *corners
    )
    for i, s in enumerate(near_spans[4:]):
        send_near(s, near[near_spans[i + 2]], x1h)
    for s in near_spans[3:4]:
        send_on(s, x1h)
    panels = jax.ShapeDtypeStruct((slots, size, 2 * size), BF16)
    rows_gate = [d[s] for d, k in ((on, near_spans[2:3]),) for s in k]
    rows = vmem_call(row_factor, panels, [], "rows")(after(x0h, *rows_gate), x0m, x1h, x1m, u01, *corners)
    def parts(ways, base, width):
        found = []
        for row, pieces in ways.items():
            for (start, count), array in sorted(pieces.items(), key=lambda item: item[0]):
                array, shift = array if isinstance(array, tuple) else (array, 0)
                lo, hi = max(start, base), min(start + count, base + width)
                if lo < hi:
                    found.append((row, array, shift + lo - start, hi - lo))
        return found

    out = None
    waiting = [s for s in near_spans if s not in on]
    for base, width in spans(widths):
        top, bottom = parts(top_ways, base, width), parts(bottom_ways, base, width)
        out = update_chunk(base, width, slab0, slab1, top, bottom, x0h, x0m, x1h, x1m, u01, rows, out)
        for s in waiting[:1]:
            near[s], out = lax.optimization_barrier((near[s], out))
            send_on(s)
        waiting = waiting[1:]
    return out.reshape(slots, 1, size, cols, 1, size)


def solution(mesh):
    spec = P(None, "row", None, None, "col", None)
    return jax.shard_map(local, mesh=mesh, in_specs=(spec,), out_specs=spec, check_vma=False)
```
